256 devices in a mesh: row: 32 (over x, z_hi, core), col: 8 (over y, z_lo).
Axes of the slice: x: 4, y: 4, z: 8 (z_hi: 4, z_lo: 2; z = z_hi * 2 + z_lo), core: 2. Of those that a mesh axis runs over, the one named last changes fastest.
Arguments:
- ancestor_inverse: bfloat16 [24576, 8, 3072], P('row', 'col'), may hold values from -6 to 6
- parent_panel: bfloat16 [24576, 1024], P(('row', 'col')), may hold values from -0.15625 to 0.15625
- parent_diag_inv: bfloat16 [1024, 1024], replicated, may hold values from -1.5 to 1.5, as said below
- child_panel_anc: bfloat16 [24576, 1024], P(('row', 'col')), may hold values from -0.15625 to 0.15625
- child_panel_par: bfloat16 [1024, 1024], replicated, may hold values from -0.1875 to 0.1875
- child_diag_inv: bfloat16 [1024, 1024], replicated, may hold values from -1.5 to 1.5, as said below
Outputs:
- ainv_ap: float32 [24576, 1024], P(('row', 'col'))
- ainv_pp: float32 [1024, 1024], P(('row', 'col'))
- ainv_ac: float32 [24576, 1024], P(('row', 'col'))
- ainv_pc: float32 [1024, 1024], P(('row', 'col'))
- ainv_cc: float32 [1024, 1024], P(('row', 'col'))
The draws below stay inside these ranges and needn't reach their ends.
Inputs may be any that keep to these rules, and one draw needn't show every extreme that they name: `parent_diag_inv`: lower triangular, with diagonal entries between 0.5 and 1.5. `child_diag_inv`: lower triangular, with diagonal entries between 0.5 and 1.5.
All inputs are finite; a program needn't handle non-finite values.
Results may differ from the reference program's by a relative error of at most 0.0041.
Values may be sent and summed in bfloat16 or wider, within the bound.
No kernel may reach another device: no remote copies, remote signals or barrier semaphores. Data moves between devices by JAX's collectives and lax.ppermute only.
A program may use at most 128 MiB of HBM per device.

```python
import jax
import jax.numpy as jnp

W = 1024
NA = 24576
BLK = 96
N_ROW = 32
N_COL = 8


def lower_factor(key):
    width_scale = 1.0 / jnp.sqrt(jnp.float32(W))
    noise = jnp.clip(jax.random.normal(jax.random.fold_in(key, 3), (W, W), jnp.float32), -4.0, 4.0) * (0.5 * width_scale)
    row_common = jnp.clip(jax.random.normal(jax.random.fold_in(key, 7), (W,), jnp.float32), -3.0, 3.0)
    col_factor = jax.random.uniform(jax.random.fold_in(key, 9), (W,), jnp.float32, 0.7, 1.3)
    strength = 0.6 * width_scale
    common = strength * row_common[:, None] * col_factor[None, :]
    diagonal = jax.random.uniform(jax.random.fold_in(key, 5), (W,), jnp.float32, 0.5, 1.5)
    return (jnp.tril(noise + common, -1) + jnp.diag(diagonal)).astype(jnp.bfloat16)


def draw_parent_diag_inv(key, part):
    return lower_factor(jax.random.fold_in(key, 11))


def draw_child_diag_inv(key, part):
    return lower_factor(jax.random.fold_in(key, 23))


def with_spikes(values, own_key, source, target, shards_of, factor):
    owner, partner = [(jnp.arange(values.shape[position]) // (values.shape[position] // shards_of)).reshape([-1 if axis == position else 1 for axis in range(values.ndim)]) for position in (source, target)]
    chosen = jax.random.permutation(own_key, shards_of)[partner]
    strong = (owner == chosen) | (owner == (partner + shards_of // 2) % shards_of)
    return jnp.where(strong, factor * values, values)


def shard_levels(key, extent, shards, low, top_value):
    factor_of = 1.0
    for axis_at, blocks in shards:
        steps = jax.random.uniform(jax.random.fold_in(jax.random.fold_in(key, 6), axis_at), (blocks,), jnp.float32, low / len(shards), top_value / len(shards))
        factor_of = factor_of * jnp.repeat(jnp.exp(steps), extent[axis_at] // blocks).reshape((-1,) + (1,) * (len(extent) - 1 - axis_at))
    return factor_of


def scatter_about(rng, shape, scale, bound, split=(), kind=jnp.bfloat16):
    values = scale * jax.random.normal(rng, shape, jnp.float32)
    if split:
        values = values * shard_levels(rng, shape, split, -0.22, 0.18)
    return jnp.clip(values, -bound, bound).astype(kind)


def heavy_noise(stream_key, shape, width, reach, split, heavy, kind=jnp.bfloat16):
    result = width * jax.random.normal(stream_key, shape, jnp.float32)
    if split:
        result = result * shard_levels(stream_key, shape, split, -0.22, 0.18)
    return jnp.clip(with_spikes(result, jax.random.fold_in(stream_key, 3), *heavy), -reach, reach).astype(kind)


def setup_inputs(seed: int = 0) -> dict:
    splits = jax.random.split(jax.random.key(seed), 7)
    return {
        "ancestor_inverse": scatter_about(splits[0], (NA, N_COL, NA // N_COL), 1.0, 6.0, ((0, 32), (1, 8))),
        "parent_panel": heavy_noise(splits[1], (NA, W), NA ** -0.5, 0.15625, ((0, 256),), (0, 1, 256, 6.0)),
        "parent_diag_inv": draw_parent_diag_inv(jax.random.fold_in(splits[6], 71), 0),
        "child_panel_anc": heavy_noise(splits[3], (NA, W), NA ** -0.5, 0.15625, ((0, 256),), (0, 1, 256, 6.0)),
        "child_panel_par": scatter_about(splits[4], (W, W), W ** -0.5, 0.1875),
        "child_diag_inv": draw_child_diag_inv(jax.random.fold_in(splits[6], 71), 0),
    }


def reference(ancestor_inverse, parent_panel, parent_diag_inv, child_panel_anc, child_panel_par, child_diag_inv):
    full_inverse = ancestor_inverse.reshape(NA, N_COL, N_ROW, BLK).transpose(0, 2, 1, 3).reshape(NA, NA)
    upper_prod = jnp.dot(full_inverse, parent_panel, preferred_element_type=jnp.float32)
    upper_round = upper_prod.astype(jnp.bfloat16)
    lower_first = jnp.dot(full_inverse, child_panel_anc, preferred_element_type=jnp.float32)
    shifted = jnp.dot(upper_round, child_panel_par, preferred_element_type=jnp.float32)
    shifted_round = shifted.astype(jnp.bfloat16)
    lower_prod_anc = lower_first - shifted
    anc_round = lower_prod_anc.astype(jnp.bfloat16)
    mixed_round = jnp.dot(parent_panel, child_panel_par, preferred_element_type=jnp.float32).astype(jnp.bfloat16)
    diag_prod = jnp.dot(parent_diag_inv, child_panel_par, preferred_element_type=jnp.float32).astype(jnp.bfloat16)
    ainv_pp = jnp.dot(parent_diag_inv.T, parent_diag_inv, preferred_element_type=jnp.float32) + jnp.dot(parent_panel.T, upper_round, preferred_element_type=jnp.float32)
    pp_round = ainv_pp.astype(jnp.bfloat16)
    cross = jnp.dot(upper_round.T, child_panel_anc, preferred_element_type=jnp.float32)
    lower_prod_par = jnp.dot(pp_round, child_panel_par, preferred_element_type=jnp.float32) - cross
    ainv_cc = (jnp.dot(child_diag_inv.T, child_diag_inv, preferred_element_type=jnp.float32)
               + jnp.dot(diag_prod.T, diag_prod, preferred_element_type=jnp.float32)
               + jnp.dot(child_panel_anc.T, anc_round, preferred_element_type=jnp.float32)
               + jnp.dot(mixed_round.T, shifted_round, preferred_element_type=jnp.float32)
               - jnp.dot(shifted_round.T, child_panel_anc, preferred_element_type=jnp.float32))
    return (-upper_prod, ainv_pp, -lower_prod_anc, -lower_prod_par, ainv_cc)
```

```python
import jax
import jax.numpy as jnp
from jax import lax
from jax.sharding import Mesh, PartitionSpec as P

ROW = ("x", "zh", "core")
COL = ("y", "zl")
ALL = ROW + COL
BF = jnp.bfloat16
F32 = jnp.float32


def dot(a, b, ca=1, cb=0):
    return lax.dot_general(a, b, (((ca,), (cb,)), ((), ())), preferred_element_type=F32)


def shards(z, pp, pdi, ca, cp, cdi):
    rows, w = pp.shape
    nr, nc = lax.axis_size(ROW), lax.axis_size(COL)
    sl = w // nr
    mine = sl // nc
    block = z.reshape(z.shape[0], -1)
    panels = lax.all_gather(jnp.concatenate([pp, ca], axis=1), ROW, axis=0, tiled=True)
    part = dot(block, panels).astype(BF).reshape(nc, rows, 2 * w)
    got = lax.all_to_all(part, COL, 0, 0, tiled=True)
    total = jnp.sum(got.astype(F32), axis=0)
    upper, lower = total[:, :w], total[:, w:]
    u = upper.astype(BF)
    shifted = dot(u, cp)
    s = shifted.astype(BF)
    anc = lower - shifted
    a = anc.astype(BF)

    x = jnp.stack([u.T, s.T, a.T]).reshape(3, nr, sl, rows).transpose(1, 0, 2, 3)
    x = lax.all_to_all(x, ROW, 0, 0, tiled=True)
    x = x.transpose(1, 2, 0, 3).reshape(3 * sl, nr * rows)
    g = dot(x, panels)
    g1t = g[:sl, :w]
    cross = g[:sl, w:]
    stp = g[sl : 2 * sl, :w]
    stc = g[sl : 2 * sl, w:]
    atc = g[2 * sl :, w:]
    t2 = dot(stp.astype(BF), cp) + atc
    t = jnp.stack([g1t, t2]).reshape(2, sl, nr, sl).transpose(2, 0, 3, 1)
    t = lax.all_to_all(t, ROW, 0, 0, tiled=True)
    t = t.transpose(1, 2, 0, 3).reshape(2, sl, w)
    f = jnp.stack([t[0], cross, t[1] - stc]).reshape(3, nc, mine, w).transpose(1, 0, 2, 3)
    f = lax.all_to_all(f, COL, 0, 0, tiled=True)
    f = jnp.sum(f, axis=0)

    diag_prod = dot(pdi, cp).astype(BF)
    first = (lax.axis_index(ROW) * nc + lax.axis_index(COL)) * mine
    cols = lambda m: lax.dynamic_slice_in_dim(m, first, mine, 1)
    pp_out = dot(cols(pdi), pdi, 0, 0) + f[0]
    pc = f[1] - dot(pp_out.astype(BF), cp)
    cc = dot(cols(cdi), cdi, 0, 0) + dot(cols(diag_prod), diag_prod, 0, 0) + f[2]
    return -upper, pp_out, -anc, pc, cc


def solution(mesh):
    fine = Mesh(mesh.devices.reshape(4, 4, 2, 4, 2), ALL)
    out = P(ALL, None)
    return jax.shard_map(
        shards,
        mesh=fine,
        in_specs=(P(ROW, COL, None), out, P(), out, P(), P()),
        out_specs=(out,) * 5,
        check_vma=False,
    )
```

```python
import jax
import jax.numpy as jnp
from jax import lax
from jax.experimental import pallas as pl
from jax.experimental.pallas import tpu as pltpu
from jax.sharding import Mesh, PartitionSpec as P

ROW = ("x", "zh", "core")
COL = ("y", "zl")
ALL = ROW + COL
BF = jnp.bfloat16
F32 = jnp.float32
RING = (0, 1, 3, 2)


def dot(a, b, ca=1, cb=0):
    return lax.dot_general(a, b, (((ca,), (cb,)), ((), ())), preferred_element_type=F32)


def shift(a, axis, by):
    n = lax.axis_size(axis)
    return lax.ppermute(a, axis, [(i, (i + by) % n) for i in range(n)])


def swap(a):
    return shift(a, "core", 1)


def ring(a, axis, direct=False):
    after = shift(a, axis, -1)
    before = shift(a, axis, 1)
    if direct:
        return [a, after, before, shift(a, axis, 2)]
    half = a.shape[0] // 2
    return [a, after, before, shift(after[:half], axis, -1), shift(before[half:], axis, 1)]


def product_kernel(zrows, where, *refs):
    first, second = refs[:5], refs[5:10]
    z_own, z_other, out, panel_out, panel, sem, out_sem = refs[10:]
    step = pl.program_id(0)
    steps = pl.num_programs(0)
    part1, part2 = first[3].shape[0] // 2, second[3].shape[0] // 2
    shard = part1 + part2

    def copies():
        x, zh = where[0], where[1]
        for pieces, rows, start in ((first, part1, 0), (second, part2, part1)):
            for k, outer in enumerate((0, 1, 3, 2, 2)):
                for n in range(pieces[k].shape[0] // rows):
                    inner = RING[n + (2 if k == 4 else 0)]
                    dx, dz = (outer, inner) if start == 0 else (inner, outer)
                    at = lax.rem(x + dx, 4) * 4 + lax.rem(zh + dz, 4)
                    at = pl.multiple_of(at * shard + start, 64)
                    yield pltpu.make_async_copy(
                        pieces[k].at[pl.ds(n * rows, rows)], panel.at[pl.ds(at, rows)], sem
                    )

    keep = pltpu.make_async_copy(panel, panel_out, out_sem)

    @pl.when(step == 0)
    def _():
        for copy in copies():
            copy.start()
        pltpu.make_async_copy(panel, panel, sem).wait()
        keep.start()

    def multiply(z):
        out[...] = jnp.dot(z[...], panel[...], preferred_element_type=F32).astype(BF).reshape(out.shape)

    pl.when(step < steps // 2)(lambda: multiply(z_own))
    pl.when(step >= steps // 2)(lambda: multiply(z_other))

    @pl.when(step == steps - 1)
    def _():
        keep.wait()


def product(where, first, second, z_own, z_other, rows):
    depth, width = z_own.shape[1], first[0].shape[1]
    steps, block = 4, 2 * z_own.shape[0] // 4
    dests = block // rows
    half = steps // 2
    any_ = pl.BlockSpec(memory_space=pl.ANY)
    return pl.pallas_call(
        lambda *refs: product_kernel(block, *refs),
        grid_spec=pltpu.PrefetchScalarGridSpec(
            num_scalar_prefetch=1,
            grid=(steps,),
            in_specs=[any_] * 10
            + [
                pl.BlockSpec((block, depth), lambda i, w: (jnp.minimum(i, half - 1), 0)),
                pl.BlockSpec((block, depth), lambda i, w: (jnp.maximum(i - half, 0), 0)),
            ],
            out_specs=[
                pl.BlockSpec((dests, rows, width), lambda i, w: (lax.rem(i + w[2] * half, steps), 0, 0)),
                any_,
            ],
            scratch_shapes=[
                pltpu.VMEM((depth, width), BF),
                pltpu.SemaphoreType.DMA(()),
                pltpu.SemaphoreType.DMA(()),
            ],
        ),
        out_shape=[
            jax.ShapeDtypeStruct((steps * dests, rows, width), BF),
            jax.ShapeDtypeStruct((depth, width), BF),
        ],
        compiler_params=pltpu.CompilerParams(vmem_limit_bytes=56 << 20),
        cost_estimate=pl.CostEstimate(
            flops=4 * z_own.shape[0] * depth * width,
            transcendentals=0,
            bytes_accessed=4 * z_own.size + 4 * depth * width + 4 * z_own.shape[0] * width,
        ),
    )(where, *first, *second, z_own, z_other)


def shards(z, pp, pdi, ca, cp, cdi):
    rows, w = pp.shape
    nr, nc = lax.axis_size(ROW), lax.axis_size(COL)
    sl = w // nr
    mine = sl // nc
    core = lax.axis_index("core")
    where = jnp.stack([lax.axis_index("x"), lax.axis_index("zh"), core]).astype(jnp.int32)
    block = z.reshape(z.shape[0], -1)

    even = core == 0
    got = swap(jnp.where(even, ca, pp))
    own = jnp.where(even, pp, ca)
    shard = jnp.concatenate([jnp.where(even, own, got), jnp.where(even, got, own)])
    split = 2 * shard.shape[0] // 3
    other_block = swap(block)
    along_z = jnp.concatenate(ring(shard[:split], "zh"))
    along_x = jnp.concatenate(ring(shard[split:], "x", direct=True))
    part, panel = product(where, ring(along_z, "x"), ring(along_x, "zh"), block, other_block, rows)
    other_panel = swap(panel)
    got = lax.all_to_all(part, ("core",) + COL, 0, 0, tiled=True)
    upper = jnp.sum(got[:nc].astype(F32), axis=0)
    lower = jnp.sum(got[nc:].astype(F32), axis=0)
    u = upper.astype(BF)
    shifted = dot(u, cp)
    s = shifted.astype(BF)
    anc = lower - shifted
    a = anc.astype(BF)

    x = jnp.stack([u.T, s.T, a.T]).reshape(3, nr, sl, rows).transpose(1, 0, 2, 3)
    x = lax.all_to_all(x, ROW, 0, 0, tiled=True)
    x = x.transpose(1, 2, 0, 3).reshape(3 * sl, nr * rows)
    g0, g1 = dot(x, panel), dot(x, other_panel)
    gp, gc = jnp.where(even, g0, g1), jnp.where(even, g1, g0)
    g1t, stp = gp[:sl], gp[sl : 2 * sl]
    cross, stc, atc = gc[:sl], gc[sl : 2 * sl], gc[2 * sl :]
    t2 = dot(stp.astype(BF), cp) + atc
    t = jnp.stack([g1t, t2]).reshape(2, sl, nr, sl).transpose(2, 0, 3, 1)
    t = lax.all_to_all(t, ROW, 0, 0, tiled=True)
    t = t.transpose(1, 2, 0, 3).reshape(2, sl, w)
    f = jnp.stack([t[0], cross, t[1] - stc]).reshape(3, nc, mine, w).transpose(1, 0, 2, 3)
    f = lax.all_to_all(f, COL, 0, 0, tiled=True)
    f = jnp.sum(f, axis=0)

    diag_prod = dot(pdi, cp).astype(BF)
    first = (lax.axis_index(ROW) * nc + lax.axis_index(COL)) * mine
    cols = lambda m: lax.dynamic_slice_in_dim(m, first, mine, 1)
    pp_out = dot(cols(pdi), pdi, 0, 0) + f[0]
    pc = f[1] - dot(pp_out.astype(BF), cp)
    cc = dot(cols(cdi), cdi, 0, 0) + dot(cols(diag_prod), diag_prod, 0, 0) + f[2]
    return -upper, pp_out, -anc, pc, cc


def solution(mesh):
    fine = Mesh(mesh.devices.reshape(4, 4, 2, 4, 2), ALL)
    out = P(ALL, None)
    return jax.shard_map(
        shards,
        mesh=fine,
        in_specs=(P(ROW, COL, None), out, P(), out, P(), P()),
        out_specs=(out,) * 5,
        check_vma=False,
    )
```

```python
import jax
import jax.numpy as jnp
from jax import lax
from jax.sharding import Mesh, PartitionSpec as P

ROW = ("x", "zh", "core")
COL = ("y", "zl")
ALL = ROW + COL
BF = jnp.bfloat16
F32 = jnp.float32


def dot(a, b, ca=1, cb=0):
    return lax.dot_general(a, b, (((ca,), (cb,)), ((), ())), preferred_element_type=F32)


def hold(a):
    return lax.optimization_barrier(a)


def exchange(a, axes):
    return lax.all_to_all(a, axes, 0, 0, tiled=True)


def shards(z, pp, pdi, ca, cp, cdi):
    rows, w = pp.shape
    nr, nc = lax.axis_size(ROW), lax.axis_size(COL)
    sl = w // nr
    mine = sl // nc
    block = z.reshape(z.shape[0], -1)

    def by_col(m):
        return m.reshape(-1, nr, nc, mine).transpose(0, 2, 1, 3).reshape(-1, w)

    parent = lax.all_gather(pp, ROW, axis=0, tiled=True)
    child = lax.all_gather(ca, ROW, axis=0, tiled=True)

    cp_by = by_col(cp)
    mixed = dot(pp, cp_by).astype(BF)
    wide = jnp.concatenate([mixed, ca], axis=1)
    wide = exchange(jnp.broadcast_to(wide, (nc,) + wide.shape), COL).reshape(nc * rows, 2 * w)
    mixed_by, anc_rows = wide[:, :w], wide[:, w:]
    anc_by = by_col(anc_rows)
    diag_prod = dot(pdi, cp).astype(BF)
    first = (lax.axis_index(ROW) * nc + lax.axis_index(COL)) * mine
    cols = lambda m: lax.dynamic_slice_in_dim(m, first, mine, 1)
    diag_upper = dot(cols(pdi), pdi, 0, 0)
    diag_lower = dot(cols(cdi), cdi, 0, 0) + dot(cols(diag_prod), diag_prod, 0, 0)
    parent, cp_by, mixed_by, anc_rows, anc_by, diag_upper, diag_lower = hold(
        (parent, cp_by, mixed_by, anc_rows, anc_by, diag_upper, diag_lower)
    )

    up = dot(block, parent).astype(BF)
    upper = exchange(up.reshape(nc, rows, w), COL)
    sp = dot(up, cp).astype(BF)
    sp_by = dot(up, cp_by).astype(BF)
    early = dot(mixed_by, sp, 0, 0) - dot(sp_by, anc_rows, 0, 0) - dot(anc_by, sp, 0, 0)
    upper = jnp.sum(upper.astype(F32), axis=0)
    u = upper.astype(BF)
    x = exchange(u.T.reshape(nr, sl, rows), ROW)
    shifted = dot(u, cp)
    x = hold(x.transpose(1, 0, 2).reshape(sl, nr * rows))
    t = hold(dot(parent, x, 0, 1))
    t = exchange(t.reshape(nr, sl, sl), ROW)
    child, early, t, x, shifted = hold((child, early, t, x, shifted))

    g1 = t.transpose(1, 0, 2).reshape(sl, w)
    f = jnp.stack([g1, dot(x, child)]).reshape(2, nc, mine, w).transpose(1, 0, 2, 3)
    f, child = hold((f, child))
    f = exchange(f, COL)
    lp = dot(block, child).astype(BF)
    low = (early + dot(anc_by, lp, 0, 0)).astype(BF)
    f, low = hold((f, low))
    low = exchange(low.reshape(nc, nr * mine, w), COL)
    low = jnp.sum(low.astype(F32), axis=0)
    lp, low = hold((lp, low))
    low = exchange(low.reshape(nr, mine, w), ROW)
    lower = exchange(lp.reshape(nc, rows, w), COL)
    f = jnp.sum(f, axis=0)
    lower = jnp.sum(lower.astype(F32), axis=0)
    low = jnp.sum(low, axis=0)

    pp_out = diag_upper + f[0]
    pc = f[1] - dot(pp_out.astype(BF), cp)
    cc = diag_lower + low
    return -upper, pp_out, shifted - lower, pc, cc


def solution(mesh):
    fine = Mesh(mesh.devices.reshape(4, 4, 2, 4, 2), ALL)
    out = P(ALL, None)
    return jax.shard_map(
        shards,
        mesh=fine,
        in_specs=(P(ROW, COL, None), out, P(), out, P(), P()),
        out_specs=(out,) * 5,
        check_vma=False,
    )
```

```python
import jax
import jax.numpy as jnp
from jax import lax
from jax.experimental import pallas as pl
from jax.experimental.pallas import tpu as pltpu
from jax.sharding import Mesh, PartitionSpec as P

ROW = ("x", "zh", "core")
COL = ("y", "zl")
ALL = ROW + COL
BF = jnp.bfloat16
F32 = jnp.float32
RING = (0, 1, 3, 2)


def dot(a, b, ca=1, cb=0):
    return lax.dot_general(a, b, (((ca,), (cb,)), ((), ())), preferred_element_type=F32)


def hold(a):
    return lax.optimization_barrier(a)


def exchange(a, axes):
    return lax.all_to_all(a, axes, 0, 0, tiled=True)


def shift(a, axis, by):
    n = lax.axis_size(axis)
    return lax.ppermute(a, axis, [(i, (i + by) % n) for i in range(n)])


def swap(a):
    return shift(a, "core", 1)


def ring(a, axis, direct=False):
    after = shift(a, axis, -1)
    before = shift(a, axis, 1)
    if direct:
        return [a, after, before, shift(a, axis, 2)]
    half = a.shape[0] // 2
    return [a, after, before, shift(after[:half], axis, -1), shift(before[half:], axis, 1)]


def product_kernel(where, *refs):
    mine, others = refs[:5], refs[5:10]
    z, out, panel_out, panel, sem, out_sem = refs[10:]
    step = pl.program_id(0)
    rows = mine[0].shape[0] // 4
    keep = pltpu.make_async_copy(panel, panel_out, out_sem)

    @pl.when(step == 0)
    def _():
        for pieces, core in ((mine, where[2]), (others, 1 - where[2])):
            for k, dx in enumerate((0, 1, 3, 2, 2)):
                for n in range(pieces[k].shape[0] // rows):
                    dz = RING[n + (2 if k == 4 else 0)]
                    at = lax.rem(where[0] + dx, 4) * 4 + lax.rem(where[1] + dz, 4)
                    at = pl.multiple_of((at * 2 + core) * rows, 32)
                    pltpu.make_async_copy(
                        pieces[k].at[pl.ds(n * rows, rows)], panel.at[pl.ds(at, rows)], sem
                    ).start()
        pltpu.make_async_copy(panel, panel, sem).wait()
        keep.start()

    out[...] = jnp.dot(z[...], panel[...], preferred_element_type=F32).astype(BF).reshape(out.shape)

    @pl.when(step == pl.num_programs(0) - 1)
    def _():
        keep.wait()


def product(where, mine, others, z, rows):
    depth, width = z.shape[1], mine[0].shape[1]
    steps = 2
    block = z.shape[0] // steps
    any_ = pl.BlockSpec(memory_space=pl.ANY)
    return pl.pallas_call(
        product_kernel,
        grid_spec=pltpu.PrefetchScalarGridSpec(
            num_scalar_prefetch=1,
            grid=(steps,),
            in_specs=[any_] * 10 + [pl.BlockSpec((block, depth), lambda i, w: (i, 0))],
            out_specs=[pl.BlockSpec((block // rows, rows, width), lambda i, w: (i, 0, 0)), any_],
            scratch_shapes=[
                pltpu.VMEM((depth, width), BF),
                pltpu.SemaphoreType.DMA(()),
                pltpu.SemaphoreType.DMA(()),
            ],
        ),
        out_shape=[
            jax.ShapeDtypeStruct((z.shape[0] // rows, rows, width), BF),
            jax.ShapeDtypeStruct((depth, width), BF),
        ],
        compiler_params=pltpu.CompilerParams(vmem_limit_bytes=48 << 20),
        cost_estimate=pl.CostEstimate(
            flops=2 * z.size * width,
            transcendentals=0,
            bytes_accessed=2 * z.size + 6 * depth * width + 2 * z.shape[0] * width,
        ),
    )(where, *mine, *others, z)


def shards(z, pp, pdi, ca, cp, cdi):
    rows, w = pp.shape
    nr, nc = lax.axis_size(ROW), lax.axis_size(COL)
    sl = w // nr
    own = sl // nc
    where = jnp.stack([lax.axis_index(a) for a in ROW]).astype(jnp.int32)
    block = z.reshape(z.shape[0], -1)

    child = lax.all_gather(ca, ROW, axis=0, tiled=True)
    pieces = ring(jnp.concatenate(ring(pp, "zh", direct=True)), "x")
    others = [swap(p) for p in pieces]

    diag_prod = dot(pdi, cp).astype(BF)
    first = (lax.axis_index(ROW) * nc + lax.axis_index(COL)) * own
    cols = lambda m: lax.dynamic_slice_in_dim(m, first, own, 1)
    diag_upper = dot(cols(pdi), pdi, 0, 0)
    diag_lower = dot(cols(cdi), cdi, 0, 0) + dot(cols(diag_prod), diag_prod, 0, 0)
    others[-1], diag_upper, diag_lower = hold((others[-1], diag_upper, diag_lower))

    up, parent = product(where, pieces, others, block, rows)
    upper = jnp.sum(exchange(up, COL).astype(F32), axis=0)
    u = upper.astype(BF)
    shifted = dot(u, cp)
    s = shifted.astype(BF)

    lp = dot(block, child).astype(BF).reshape(nc, rows, w)
    lower = jnp.sum(exchange(lp, COL).astype(F32), axis=0)
    anc = lower - shifted
    a = anc.astype(BF)

    x = jnp.stack([u.T, s.T, a.T]).reshape(3, nr, sl, rows).transpose(1, 0, 2, 3)
    x = exchange(x, ROW)
    x = x.transpose(1, 2, 0, 3).reshape(3 * sl, nr * rows)
    gp, gc = dot(x[: 2 * sl], parent), dot(x, child)
    g1t, stp = gp[:sl], gp[sl:]
    cross, stc, atc = gc[:sl], gc[sl : 2 * sl], gc[2 * sl :]
    t2 = dot(stp.astype(BF), cp) + atc
    t = jnp.stack([g1t, t2]).reshape(2, sl, nr, sl).transpose(2, 0, 3, 1)
    t = exchange(t, ROW)
    t = t.transpose(1, 2, 0, 3).reshape(2, sl, w)
    f = jnp.stack([t[0], cross, t[1] - stc]).reshape(3, nc, own, w).transpose(1, 0, 2, 3)
    f = jnp.sum(exchange(f, COL), axis=0)

    pp_out = diag_upper + f[0]
    pc = f[1] - dot(pp_out.astype(BF), cp)
    cc = diag_lower + f[2]
    return -upper, pp_out, -anc, pc, cc


def solution(mesh):
    fine = Mesh(mesh.devices.reshape(4, 4, 2, 4, 2), ALL)
    out = P(ALL, None)
    return jax.shard_map(
        shards,
        mesh=fine,
        in_specs=(P(ROW, COL, None), out, P(), out, P(), P()),
        out_specs=(out,) * 5,
        check_vma=False,
    )
```

```python
import jax
import jax.numpy as jnp
from jax import lax
from jax.experimental import pallas as pl
from jax.experimental.pallas import tpu as pltpu
from jax.sharding import Mesh, PartitionSpec as P

ROW = ("x", "zh", "core")
COL = ("y", "zl")
ALL = ROW + COL
BF = jnp.bfloat16
F32 = jnp.float32
RING = (0, 1, 3, 2)


def dot(a, b, ca=1, cb=0):
    return lax.dot_general(a, b, (((ca,), (cb,)), ((), ())), preferred_element_type=F32)


def hold(a):
    return lax.optimization_barrier(a)


def exchange(a, axes):
    return lax.all_to_all(a, axes, 0, 0, tiled=True)


def shift(a, axis, by):
    n = lax.axis_size(axis)
    return lax.ppermute(a, axis, [(i, (i + by) % n) for i in range(n)])


def swap(a):
    return shift(a, "core", 1)


def ring(a, axis, direct=False):
    after = shift(a, axis, -1)
    before = shift(a, axis, 1)
    if direct:
        return [a, after, before, shift(a, axis, 2)]
    half = a.shape[0] // 2
    return [a, after, before, shift(after[:half], axis, -1), shift(before[half:], axis, 1)]


def lay_out(where, mine, others, panel, sems):
    rows = mine[0].shape[0] // 4
    for k, dx in enumerate((0, 1, 3, 2, 2)):
        for pieces, core in ((mine, where[2]), (others, 1 - where[2])):
            for n in range(pieces[k].shape[0] // rows):
                dz = RING[n + (2 if k == 4 else 0)]
                at = lax.rem(where[0] + dx, 4) * 4 + lax.rem(where[1] + dz, 4)
                at = pl.multiple_of((at * 2 + core) * rows, 32)
                pltpu.make_async_copy(
                    pieces[k].at[pl.ds(n * rows, rows)],
                    panel.at[pl.ds(at, rows)],
                    sems.at[RING.index(dx)],
                ).start()


def ring_block(step, where):
    return lax.rem(where[0] + jnp.where(step < 2, step, 5 - step), 4)


def product_kernel(where, *refs):
    z, out, panel, zcols, acc, result, sems, zsems, out_sem = refs[10:]
    depth = panel.shape[0] // 4

    def block(step):
        return pl.ds(pl.multiple_of(ring_block(step, where) * depth, 256), depth)

    zcopies = [
        pltpu.make_async_copy(z.at[:, block(step)], zcols.at[step], zsems.at[step]) for step in range(4)
    ]
    for copy in zcopies:
        copy.start()
    lay_out(where, refs[:5], refs[5:10], panel, sems)
    for step in range(4):
        part = panel.at[block(step)]
        zcopies[step].wait()
        pltpu.make_async_copy(part, part, sems.at[step]).wait()
        got = jnp.dot(zcols[step], part[...], preferred_element_type=F32)
        if step == 0:
            acc[...] = got
        elif step < 3:
            acc[...] += got
        else:
            result[...] = (acc[...] + got).astype(BF).reshape(result.shape)
    copy = pltpu.make_async_copy(result, out, out_sem)
    copy.start()
    copy.wait()


def product(where, mine, others, z, rows):
    depth, width = z.shape[1], mine[0].shape[1]
    hbm = pl.BlockSpec(memory_space=pltpu.HBM)
    blocks = (z.shape[0] // rows, rows, width)
    return pl.pallas_call(
        product_kernel,
        grid_spec=pltpu.PrefetchScalarGridSpec(
            num_scalar_prefetch=1,
            grid=(),
            in_specs=[hbm] * 11,
            out_specs=hbm,
            scratch_shapes=[
                pltpu.VMEM((depth, width), BF),
                pltpu.VMEM((4, z.shape[0], depth // 4), BF),
                pltpu.VMEM((z.shape[0], width), F32),
                pltpu.VMEM(blocks, BF),
                pltpu.SemaphoreType.DMA((4,)),
                pltpu.SemaphoreType.DMA((4,)),
                pltpu.SemaphoreType.DMA(()),
            ],
        ),
        out_shape=jax.ShapeDtypeStruct(blocks, BF),
        compiler_params=pltpu.CompilerParams(vmem_limit_bytes=60 << 20),
        cost_estimate=pl.CostEstimate(
            flops=2 * z.size * width,
            transcendentals=0,
            bytes_accessed=2 * z.size + 2 * depth * width + 2 * z.shape[0] * width,
        ),
    )(where, *mine, *others, z)


def panel_kernel(where, *refs):
    out, panel, sems, out_sem = refs[10:]
    depth = panel.shape[0] // 4
    lay_out(where, refs[:5], refs[5:10], panel, sems)
    copies = []
    for step in range(4):
        at = pl.ds(pl.multiple_of(ring_block(step, where) * depth, 256), depth)
        pltpu.make_async_copy(panel.at[at], panel.at[at], sems.at[step]).wait()
        copies.append(pltpu.make_async_copy(panel.at[at], out.at[at], out_sem.at[step]))
        copies[-1].start()
    for copy in copies:
        copy.wait()


def whole_panel(where, mine, others, depth):
    width = mine[0].shape[1]
    hbm = pl.BlockSpec(memory_space=pltpu.HBM)
    return pl.pallas_call(
        panel_kernel,
        grid_spec=pltpu.PrefetchScalarGridSpec(
            num_scalar_prefetch=1,
            grid=(),
            in_specs=[hbm] * 10,
            out_specs=hbm,
            scratch_shapes=[
                pltpu.VMEM((depth, width), BF),
                pltpu.SemaphoreType.DMA((4,)),
                pltpu.SemaphoreType.DMA((4,)),
            ],
        ),
        out_shape=jax.ShapeDtypeStruct((depth, width), BF),
        compiler_params=pltpu.CompilerParams(vmem_limit_bytes=60 << 20),
        cost_estimate=pl.CostEstimate(flops=0, transcendentals=0, bytes_accessed=4 * depth * width),
    )(where, *mine, *others)


def shards(z, pp, pdi, ca, cp, cdi):
    rows, w = pp.shape
    nr, nc = lax.axis_size(ROW), lax.axis_size(COL)
    sl = w // nr
    own = sl // nc
    where = jnp.stack([lax.axis_index(a) for a in ROW]).astype(jnp.int32)
    block = z.reshape(z.shape[0], -1)

    child = lax.all_gather(ca, ROW, axis=0, tiled=True)
    pieces = ring(jnp.concatenate(ring(pp, "zh", direct=True)), "x")
    others = [swap(p) for p in pieces]

    diag_prod = dot(pdi, cp).astype(BF)
    first = (lax.axis_index(ROW) * nc + lax.axis_index(COL)) * own
    cols = lambda m: lax.dynamic_slice_in_dim(m, first, own, 1)
    diag_upper = dot(cols(pdi), pdi, 0, 0)
    diag_lower = dot(cols(cdi), cdi, 0, 0) + dot(cols(diag_prod), diag_prod, 0, 0)
    others[-1], diag_upper, diag_lower = hold((others[-1], diag_upper, diag_lower))

    up = product(where, pieces, others, block, rows)
    upper = jnp.sum(exchange(up, COL).astype(F32), axis=0)
    u = upper.astype(BF)
    shifted = dot(u, cp)
    s = shifted.astype(BF)

    lp = dot(block, child).astype(BF).reshape(nc, rows, w)
    others[0], lp = hold((others[0], lp))
    parent = whole_panel(where, pieces, others, block.shape[1])
    lower = jnp.sum(exchange(lp, COL).astype(F32), axis=0)
    anc = lower - shifted
    a = anc.astype(BF)

    x = jnp.stack([u.T, s.T, a.T]).reshape(3, nr, sl, rows).transpose(1, 0, 2, 3)
    x = exchange(x, ROW)
    x = x.transpose(1, 2, 0, 3).reshape(3 * sl, nr * rows)
    gp, gc = dot(x[: 2 * sl], parent), dot(x, child)
    g1t, stp = gp[:sl], gp[sl:]
    cross, stc, atc = gc[:sl], gc[sl : 2 * sl], gc[2 * sl :]
    t2 = dot(stp.astype(BF), cp) + atc
    t = jnp.stack([g1t, t2]).reshape(2, sl, nr, sl).transpose(2, 0, 3, 1)
    t = exchange(t, ROW)
    t = t.transpose(1, 2, 0, 3).reshape(2, sl, w)
    f = jnp.stack([t[0], cross, t[1] - stc]).reshape(3, nc, own, w).transpose(1, 0, 2, 3)
    f = jnp.sum(exchange(f, COL), axis=0)

    pp_out = diag_upper + f[0]
    pc = f[1] - dot(pp_out.astype(BF), cp)
    cc = diag_lower + f[2]
    return -upper, pp_out, -anc, pc, cc


def solution(mesh):
    fine = Mesh(mesh.devices.reshape(4, 4, 2, 4, 2), ALL)
    out = P(ALL, None)
    return jax.shard_map(
        shards,
        mesh=fine,
        in_specs=(P(ROW, COL, None), out, P(), out, P(), P()),
        out_specs=(out,) * 5,
        check_vma=False,
    )
```

```python
import jax
import jax.numpy as jnp
from jax import lax
from jax.experimental import pallas as pl
from jax.experimental.pallas import tpu as pltpu
from jax.sharding import Mesh, PartitionSpec as P

ROW = ("x", "zh", "core")
COL = ("y", "zl")
ALL = ROW + COL
BF = jnp.bfloat16
F32 = jnp.float32
RING = (0, 1, 3, 2)


def dot(a, b, ca=1, cb=0):
    return lax.dot_general(a, b, (((ca,), (cb,)), ((), ())), preferred_element_type=F32)


def hold(a):
    return lax.optimization_barrier(a)


def exchange(a, axes):
    return lax.all_to_all(a, axes, 0, 0, tiled=True)


def shift(a, axis, by):
    n = lax.axis_size(axis)
    return lax.ppermute(a, axis, [(i, (i + by) % n) for i in range(n)])


def swap(a):
    return shift(a, "core", 1)


def ring(a, axis):
    return [a, shift(a, axis, -1), shift(a, axis, 1), shift(a, axis, 2)]


def lay_out(where, mine, others, panel, sems):
    rows = mine[0].shape[0] // 4
    for k, dx in enumerate((0, 1, 3, 2, 2)):
        for pieces, core in ((mine, where[2]), (others, 1 - where[2])):
            for n in range(pieces[k].shape[0] // rows):
                dz = RING[n + (2 if k == 4 else 0)]
                at = lax.rem(where[0] + dx, 4) * 4 + lax.rem(where[1] + dz, 4)
                at = pl.multiple_of((at * 2 + core) * rows, 32)
                pltpu.make_async_copy(
                    pieces[k].at[pl.ds(n * rows, rows)],
                    panel.at[pl.ds(at, rows)],
                    sems.at[RING.index(dx)],
                ).start()


def ring_block(step, where):
    return lax.rem(where[0] + jnp.where(step < 2, step, 5 - step), 4)


def product_kernel(where, *refs):
    z, out, panel, zcols, acc, result, sems, zsems, out_sem = refs[10:]
    depth = panel.shape[0] // 4

    def block(step):
        return pl.ds(pl.multiple_of(ring_block(step, where) * depth, 256), depth)

    zcopies = [
        pltpu.make_async_copy(z.at[:, block(step)], zcols.at[step], zsems.at[step]) for step in range(4)
    ]
    for copy in zcopies:
        copy.start()
    lay_out(where, refs[:5], refs[5:10], panel, sems)
    for step in range(4):
        part = panel.at[block(step)]
        zcopies[step].wait()
        pltpu.make_async_copy(part, part, sems.at[step]).wait()
        got = jnp.dot(zcols[step], part[...], preferred_element_type=F32)
        if step == 0:
            acc[...] = got
        elif step < 3:
            acc[...] += got
        else:
            result[...] = (acc[...] + got).astype(BF).reshape(result.shape)
    copy = pltpu.make_async_copy(result, out, out_sem)
    copy.start()
    copy.wait()


def product(where, mine, others, z, rows):
    depth, width = z.shape[1], mine[0].shape[1]
    hbm = pl.BlockSpec(memory_space=pltpu.HBM)
    blocks = (z.shape[0] // rows, rows, width)
    return pl.pallas_call(
        product_kernel,
        grid_spec=pltpu.PrefetchScalarGridSpec(
            num_scalar_prefetch=1,
            grid=(),
            in_specs=[hbm] * 11,
            out_specs=hbm,
            scratch_shapes=[
                pltpu.VMEM((depth, width), BF),
                pltpu.VMEM((4, z.shape[0], depth // 4), BF),
                pltpu.VMEM((z.shape[0], width), F32),
                pltpu.VMEM(blocks, BF),
                pltpu.SemaphoreType.DMA((4,)),
                pltpu.SemaphoreType.DMA((4,)),
                pltpu.SemaphoreType.DMA(()),
            ],
        ),
        out_shape=jax.ShapeDtypeStruct(blocks, BF),
        compiler_params=pltpu.CompilerParams(vmem_limit_bytes=60 << 20),
        cost_estimate=pl.CostEstimate(
            flops=2 * z.size * width,
            transcendentals=0,
            bytes_accessed=2 * z.size + 2 * depth * width + 2 * z.shape[0] * width,
        ),
    )(where, *mine, *others, z)


def panel_kernel(where, *refs):
    out, panel, sems, out_sem = refs[10:]
    depth = panel.shape[0] // 4
    lay_out(where, refs[:5], refs[5:10], panel, sems)
    copies = []
    for step in range(4):
        at = pl.ds(pl.multiple_of(ring_block(step, where) * depth, 256), depth)
        pltpu.make_async_copy(panel.at[at], panel.at[at], sems.at[step]).wait()
        copies.append(pltpu.make_async_copy(panel.at[at], out.at[at], out_sem.at[step]))
        copies[-1].start()
    for copy in copies:
        copy.wait()


def whole_panel(where, mine, others, depth):
    width = mine[0].shape[1]
    hbm = pl.BlockSpec(memory_space=pltpu.HBM)
    return pl.pallas_call(
        panel_kernel,
        grid_spec=pltpu.PrefetchScalarGridSpec(
            num_scalar_prefetch=1,
            grid=(),
            in_specs=[hbm] * 10,
            out_specs=hbm,
            scratch_shapes=[
                pltpu.VMEM((depth, width), BF),
                pltpu.SemaphoreType.DMA((4,)),
                pltpu.SemaphoreType.DMA((4,)),
            ],
        ),
        out_shape=jax.ShapeDtypeStruct((depth, width), BF),
        compiler_params=pltpu.CompilerParams(vmem_limit_bytes=60 << 20),
        cost_estimate=pl.CostEstimate(flops=0, transcendentals=0, bytes_accessed=4 * depth * width),
    )(where, *mine, *others)


def slices_kernel(x, parent, child, cp, t, r, xt, pbuf, cbuf, cpbuf, big, psem, csem, cpsem):
    nr, kinds, sl, rows = x.shape
    depth, w = parent.shape
    parts = psem.shape[0]
    chunk = depth // parts
    copies = []
    for n in range(parts):
        at = pl.ds(n * chunk, chunk)
        copies.append((pltpu.make_async_copy(parent.at[at], pbuf.at[at], psem.at[n]), pltpu.make_async_copy(child.at[at], cbuf.at[at], csem.at[n])))
        for c in copies[-1]:
            c.start()
    ccopy = pltpu.make_async_copy(cp, cpbuf, cpsem)
    ccopy.start()
    for s in range(nr):
        xt[:, s * rows : (s + 1) * rows] = x[s].reshape(kinds * sl, rows)
    for n in range(parts):
        at = pl.ds(n * chunk, chunk)
        for c in copies[n]:
            c.wait()
        lhs = xt[:, n * chunk : (n + 1) * chunk]
        gp = jnp.dot(lhs[: 2 * sl], pbuf[at, :], preferred_element_type=F32)
        gc = jnp.dot(lhs, cbuf[at, :], preferred_element_type=F32)
        if n == 0:
            big[: 2 * sl] = gp
            big[2 * sl :] = gc
        else:
            big[: 2 * sl] += gp
            big[2 * sl :] += gc
    ccopy.wait()
    r[0] = big[2 * sl : 3 * sl]
    r[1] = big[3 * sl : 4 * sl]
    t2 = jnp.dot(big[sl : 2 * sl].astype(BF), cpbuf[...], preferred_element_type=F32) + big[4 * sl :]
    big[sl : 2 * sl] = t2
    lane = lax.broadcasted_iota(jnp.int32, (16, 128), 1) // sl
    for q in range(w // 128):
        for d in range(4):
            out = None
            for g in range(4):
                v = big[g * 16 : (g + 1) * 16, q * 128 : (q + 1) * 128]
                v = pltpu.roll(v, ((g - d) * sl) % 128, 1) if g != d else v
                out = v if out is None else jnp.where(lane == g, v, out)
            t[q * 4 + d] = out

def slices(x, parent, child, cp):
    nr, kinds, sl, rows = x.shape
    depth, w = parent.shape
    parts = 4
    any_ = pl.BlockSpec(memory_space=pl.ANY)
    vm = pl.BlockSpec(memory_space=pltpu.VMEM)
    return pl.pallas_call(
        slices_kernel,
        in_specs=[vm, any_, any_, any_],
        out_specs=[vm, vm],
        out_shape=[jax.ShapeDtypeStruct((nr, 16, 128), F32), jax.ShapeDtypeStruct((2, sl, w), F32)],
        scratch_shapes=[pltpu.VMEM((kinds * sl, depth), BF), pltpu.VMEM((depth, w), BF), pltpu.VMEM((depth, w), BF), pltpu.VMEM(cp.shape, BF), pltpu.VMEM((5 * sl, w), F32),
            pltpu.SemaphoreType.DMA((parts,)), pltpu.SemaphoreType.DMA((parts,)), pltpu.SemaphoreType.DMA(())],
        compiler_params=pltpu.CompilerParams(vmem_limit_bytes=60 << 20),
        cost_estimate=pl.CostEstimate(flops=10 * sl * depth * w, transcendentals=0, bytes_accessed=4 * depth * w),
    )(x, parent, child, cp)

def rows_kernel(t, r, f, both):
    nr = t.shape[0]
    sl = r.shape[1]
    w = r.shape[2]
    for q in range(nr // 4):
        for kind in range(2):
            tall = []
            for d in range(4):
                for h in range(2):
                    v = t[q * 4 + d]
                    g = kind * 2 + h
                    tall.append(pltpu.roll(v, (128 - g * sl) % 128, 1) if g else v)
            tall = jnp.concatenate(tall, axis=0)
            both[kind, :, q * 128 : (q + 1) * 128] = tall.T[:sl]
    nc = f.shape[0]
    own = sl // nc
    half = w // 2
    for c in range(nc):
        at = slice(c * own, (c + 1) * own)
        low = both[1, at, :] - r[1, at, :]
        f[c, :own, :w] = both[0, at, :]
        f[c, own:, :w] = r[0, at, :]
        f[c, :own, w:] = low[:, :half]
        f[c, own:, w:] = low[:, half:]

def rows_of(t, r, nc):
    sl, w = r.shape[1:]
    vm = pl.BlockSpec(memory_space=pltpu.VMEM)
    return pl.pallas_call(
        rows_kernel, in_specs=[vm, vm], out_specs=vm,
        out_shape=jax.ShapeDtypeStruct((nc, 2 * sl // nc, 3 * w // 2), F32),
        scratch_shapes=[pltpu.VMEM((2, sl, w), F32)],
        compiler_params=pltpu.CompilerParams(vmem_limit_bytes=16 << 20),
        cost_estimate=pl.CostEstimate(flops=0, transcendentals=0, bytes_accessed=20 * sl * w),
    )(t, r)


def shards(z, pp, pdi, ca, cp, cdi):
    rows, w = pp.shape
    nr, nc = lax.axis_size(ROW), lax.axis_size(COL)
    sl = w // nr
    own = sl // nc
    where = jnp.stack([lax.axis_index(a) for a in ROW]).astype(jnp.int32)
    block = z.reshape(z.shape[0], -1)

    child = lax.all_gather(ca, ROW, axis=0, tiled=True)
    diag_prod = dot(pdi, cp).astype(BF)
    first = (lax.axis_index(ROW) * nc + lax.axis_index(COL)) * own
    cols = lambda m: lax.dynamic_slice_in_dim(m, first, own, 1)
    diag_upper = dot(cols(pdi), pdi, 0, 0)
    diag_lower = dot(cols(cdi), cdi, 0, 0) + dot(cols(diag_prod), diag_prod, 0, 0)

    here = jnp.concatenate(ring(pp, "zh"))
    here, diag_upper, diag_lower = hold((here, diag_upper, diag_lower))
    after, before, here_other = hold((shift(here, "x", -1), shift(here, "x", 1), swap(here)))
    half = here.shape[0] // 2
    far = shift(after[:half], "x", -1), shift(before[half:], "x", 1), swap(after), swap(before)
    far_top, far_bottom, after_other, before_other = hold(far)
    pieces = [here, after, before, far_top, far_bottom]
    others = [here_other, after_other, before_other, swap(far_top), swap(far_bottom)]

    up = product(where, pieces, others, block, rows)
    upper = jnp.sum(exchange(up, COL).astype(F32), axis=0)
    u = upper.astype(BF)
    shifted = dot(u, cp)
    s = shifted.astype(BF)

    lp = dot(block, child).astype(BF).reshape(nc, rows, w)
    others[0], lp = hold((others[0], lp))
    parent = whole_panel(where, pieces, others, block.shape[1])
    lower = jnp.sum(exchange(lp, COL).astype(F32), axis=0)
    anc = lower - shifted
    a = anc.astype(BF)

    x = jnp.stack([u.T, s.T, a.T]).reshape(3, nr, sl, rows).transpose(1, 0, 2, 3)
    x = exchange(x, ROW)
    t, r = slices(x, parent, child, cp)
    t = exchange(t, ROW)
    f = jnp.sum(exchange(rows_of(t, r, nc), COL), axis=0)

    pp_out = diag_upper + f[:own, :w]
    pc = f[own:, :w] - dot(pp_out.astype(BF), cp)
    cc = diag_lower + jnp.concatenate([f[:own, w:], f[own:, w:]], axis=1)
    return -upper, pp_out, -anc, pc, cc


def solution(mesh):
    fine = Mesh(mesh.devices.reshape(4, 4, 2, 4, 2), ALL)
    out = P(ALL, None)
    return jax.shard_map(
        shards,
        mesh=fine,
        in_specs=(P(ROW, COL, None), out, P(), out, P(), P()),
        out_specs=(out,) * 5,
        check_vma=False,
    )
```

```python
import jax
import jax.numpy as jnp
from jax import lax
from jax.experimental import pallas as pl
from jax.experimental.pallas import tpu as pltpu
from jax.sharding import Mesh, PartitionSpec as P

ROW = ("x", "zh", "core")
COL = ("y", "zl")
ALL = ROW + COL
BF = jnp.bfloat16
F32 = jnp.float32
RING = (0, 1, 3, 2)


def dot(a, b, ca=1, cb=0):
    return lax.dot_general(a, b, (((ca,), (cb,)), ((), ())), preferred_element_type=F32)


def hold(a):
    return lax.optimization_barrier(a)


def exchange(a, axes):
    return lax.all_to_all(a, axes, 0, 0, tiled=True)


def shift(a, axis, by):
    n = lax.axis_size(axis)
    return lax.ppermute(a, axis, [(i, (i + by) % n) for i in range(n)])


def swap(a):
    return shift(a, "core", 1)


def ring(a, axis):
    return [a, shift(a, axis, -1), shift(a, axis, 1), shift(a, axis, 2)]


def lay_out(where, mine, others, panel, sems):
    rows = mine[0].shape[0] // 4
    for k, dx in enumerate(RING):
        for pieces, core in ((mine, where[2]), (others, 1 - where[2])):
            for n, dz in enumerate(RING):
                at = lax.rem(where[0] + dx, 4) * 4 + lax.rem(where[1] + dz, 4)
                at = pl.multiple_of((at * 2 + core) * rows, 32)
                pltpu.make_async_copy(
                    pieces[k].at[pl.ds(n * rows, rows)],
                    panel.at[pl.ds(at, rows)],
                    sems.at[k],
                ).start()


def ring_block(step, where):
    return lax.rem(where[0] + jnp.where(step < 2, step, 5 - step), 4)


def product_kernel(where, *refs):
    z, out, whole, panel, zcols, acc, result, sems, zsems, whole_sems, out_sem = refs[8:]
    depth = panel.shape[0] // 4

    def block(step):
        return pl.ds(pl.multiple_of(ring_block(step, where) * depth, 256), depth)

    zcopies = [
        pltpu.make_async_copy(z.at[:, block(step)], zcols.at[step], zsems.at[step]) for step in range(4)
    ]
    keeps = [
        pltpu.make_async_copy(panel.at[block(step)], whole.at[block(step)], whole_sems.at[step])
        for step in range(4)
    ]
    for copy in zcopies:
        copy.start()
    lay_out(where, refs[:4], refs[4:8], panel, sems)
    for step in range(4):
        part = panel.at[block(step)]
        zcopies[step].wait()
        pltpu.make_async_copy(part, part, sems.at[step]).wait()
        keeps[step].start()
        got = jnp.dot(zcols[step], part[...], preferred_element_type=F32)
        if step == 0:
            acc[...] = got
        elif step < 3:
            acc[...] += got
        else:
            result[...] = (acc[...] + got).astype(BF).reshape(result.shape)
    copy = pltpu.make_async_copy(result, out, out_sem)
    copy.start()
    for keep in keeps:
        keep.wait()
    copy.wait()


def product(where, mine, others, z, rows):
    depth, width = z.shape[1], mine[0].shape[1]
    hbm = pl.BlockSpec(memory_space=pltpu.HBM)
    blocks = (z.shape[0] // rows, rows, width)
    return pl.pallas_call(
        product_kernel,
        grid_spec=pltpu.PrefetchScalarGridSpec(
            num_scalar_prefetch=1,
            grid=(),
            in_specs=[hbm] * 9,
            out_specs=[hbm] * 2,
            scratch_shapes=[
                pltpu.VMEM((depth, width), BF),
                pltpu.VMEM((4, z.shape[0], depth // 4), BF),
                pltpu.VMEM((z.shape[0], width), F32),
                pltpu.VMEM(blocks, BF),
                pltpu.SemaphoreType.DMA((4,)),
                pltpu.SemaphoreType.DMA((4,)),
                pltpu.SemaphoreType.DMA((4,)),
                pltpu.SemaphoreType.DMA(()),
            ],
        ),
        out_shape=[jax.ShapeDtypeStruct(blocks, BF), jax.ShapeDtypeStruct((depth, width), BF)],
        compiler_params=pltpu.CompilerParams(vmem_limit_bytes=40 << 20),
        cost_estimate=pl.CostEstimate(
            flops=2 * z.size * width,
            transcendentals=0,
            bytes_accessed=2 * z.size + 2 * depth * width + 2 * z.shape[0] * width,
        ),
    )(where, *mine, *others, z)


def slices_kernel(x, parent, child, cp, t, r, xt, pbuf, cbuf, cpbuf, big, psem, csem, cpsem):
    nr, kinds, sl, rows = x.shape
    depth, w = parent.shape
    parts = psem.shape[0]
    chunk = depth // parts
    copies = []
    for n in range(parts):
        at = pl.ds(n * chunk, chunk)
        copies.append((pltpu.make_async_copy(parent.at[at], pbuf.at[at], psem.at[n]), pltpu.make_async_copy(child.at[at], cbuf.at[at], csem.at[n])))
        for c in copies[-1]:
            c.start()
    ccopy = pltpu.make_async_copy(cp, cpbuf, cpsem)
    ccopy.start()
    for s in range(nr):
        xt[:, s * rows : (s + 1) * rows] = x[s].reshape(kinds * sl, rows)
    for n in range(parts):
        at = pl.ds(n * chunk, chunk)
        for c in copies[n]:
            c.wait()
        lhs = xt[:, n * chunk : (n + 1) * chunk]
        gp = jnp.dot(lhs[: 2 * sl], pbuf[at, :], preferred_element_type=F32)
        gc = jnp.dot(lhs, cbuf[at, :], preferred_element_type=F32)
        if n == 0:
            big[: 2 * sl] = gp
            big[2 * sl :] = gc
        else:
            big[: 2 * sl] += gp
            big[2 * sl :] += gc
    ccopy.wait()
    r[0] = big[2 * sl : 3 * sl]
    r[1] = big[3 * sl : 4 * sl]
    t2 = jnp.dot(big[sl : 2 * sl].astype(BF), cpbuf[...], preferred_element_type=F32) + big[4 * sl :]
    big[sl : 2 * sl] = t2
    lane = lax.broadcasted_iota(jnp.int32, (16, 128), 1) // sl
    for q in range(w // 128):
        for d in range(4):
            out = None
            for g in range(4):
                v = big[g * 16 : (g + 1) * 16, q * 128 : (q + 1) * 128]
                v = pltpu.roll(v, ((g - d) * sl) % 128, 1) if g != d else v
                out = v if out is None else jnp.where(lane == g, v, out)
            t[q * 4 + d] = out

def slices(x, parent, child, cp):
    nr, kinds, sl, rows = x.shape
    depth, w = parent.shape
    parts = 4
    any_ = pl.BlockSpec(memory_space=pl.ANY)
    vm = pl.BlockSpec(memory_space=pltpu.VMEM)
    return pl.pallas_call(
        slices_kernel,
        in_specs=[vm, any_, any_, any_],
        out_specs=[vm, vm],
        out_shape=[jax.ShapeDtypeStruct((nr, 16, 128), F32), jax.ShapeDtypeStruct((2, sl, w), F32)],
        scratch_shapes=[pltpu.VMEM((kinds * sl, depth), BF), pltpu.VMEM((depth, w), BF), pltpu.VMEM((depth, w), BF), pltpu.VMEM(cp.shape, BF), pltpu.VMEM((5 * sl, w), F32),
            pltpu.SemaphoreType.DMA((parts,)), pltpu.SemaphoreType.DMA((parts,)), pltpu.SemaphoreType.DMA(())],
        compiler_params=pltpu.CompilerParams(vmem_limit_bytes=60 << 20),
        cost_estimate=pl.CostEstimate(flops=10 * sl * depth * w, transcendentals=0, bytes_accessed=4 * depth * w),
    )(x, parent, child, cp)

def rows_kernel(t, r, f, both):
    nr = t.shape[0]
    sl = r.shape[1]
    w = r.shape[2]
    for q in range(nr // 4):
        for kind in range(2):
            tall = []
            for d in range(4):
                for h in range(2):
                    v = t[q * 4 + d]
                    g = kind * 2 + h
                    tall.append(pltpu.roll(v, (128 - g * sl) % 128, 1) if g else v)
            tall = jnp.concatenate(tall, axis=0)
            both[kind, :, q * 128 : (q + 1) * 128] = tall.T[:sl]
    nc = f.shape[0]
    own = sl // nc
    half = w // 2
    for c in range(nc):
        at = slice(c * own, (c + 1) * own)
        low = both[1, at, :] - r[1, at, :]
        f[c, :own, :w] = both[0, at, :]
        f[c, own:, :w] = r[0, at, :]
        f[c, :own, w:] = low[:, :half]
        f[c, own:, w:] = low[:, half:]

def rows_of(t, r, nc):
    sl, w = r.shape[1:]
    vm = pl.BlockSpec(memory_space=pltpu.VMEM)
    return pl.pallas_call(
        rows_kernel, in_specs=[vm, vm], out_specs=vm,
        out_shape=jax.ShapeDtypeStruct((nc, 2 * sl // nc, 3 * w // 2), F32),
        scratch_shapes=[pltpu.VMEM((2, sl, w), F32)],
        compiler_params=pltpu.CompilerParams(vmem_limit_bytes=16 << 20),
        cost_estimate=pl.CostEstimate(flops=0, transcendentals=0, bytes_accessed=20 * sl * w),
    )(t, r)


def ancestors_kernel(got, shifted, ut, st, anc, x):
    nr, _, sl, rows = x.shape
    low = got[0].astype(F32)
    for n in range(1, got.shape[0]):
        low += got[n].astype(F32)
    low -= shifted[...]
    anc[...] = -low
    x[:, 0] = ut[...].reshape(nr, sl, rows)
    x[:, 1] = st[...].reshape(nr, sl, rows)
    x[:, 2] = low.T.astype(BF).reshape(nr, sl, rows)


def ancestors(got, shifted, ut, st, nr):
    rows, w = shifted.shape
    vmem = pl.BlockSpec(memory_space=pltpu.VMEM)
    return pl.pallas_call(
        ancestors_kernel,
        in_specs=[vmem] * 4,
        out_specs=[vmem] * 2,
        out_shape=[
            jax.ShapeDtypeStruct((rows, w), F32),
            jax.ShapeDtypeStruct((nr, 3, w // nr, rows), BF),
        ],
        compiler_params=pltpu.CompilerParams(vmem_limit_bytes=16 << 20),
        cost_estimate=pl.CostEstimate(flops=9 * rows * w, transcendentals=0, bytes_accessed=40 * rows * w),
    )(got, shifted, ut, st)


def shards(z, pp, pdi, ca, cp, cdi):
    rows, w = pp.shape
    nr, nc = lax.axis_size(ROW), lax.axis_size(COL)
    sl = w // nr
    own = sl // nc
    where = jnp.stack([lax.axis_index(a) for a in ROW]).astype(jnp.int32)
    block = z.reshape(z.shape[0], -1)

    child = lax.all_gather(ca, ROW, axis=0, tiled=True)
    diag_prod = dot(pdi, cp).astype(BF)
    first = (lax.axis_index(ROW) * nc + lax.axis_index(COL)) * own
    cols = lambda m: lax.dynamic_slice_in_dim(m, first, own, 1)
    diag_upper = dot(cols(pdi), pdi, 0, 0)
    diag_lower = dot(cols(cdi), cdi, 0, 0) + dot(cols(diag_prod), diag_prod, 0, 0)

    here = jnp.concatenate(ring(pp, "zh"))
    here, diag_upper, diag_lower = hold((here, diag_upper, diag_lower))
    pieces = ring(here, "x")
    others = [swap(piece) for piece in pieces]

    up, parent = product(where, pieces, others, block, rows)
    upper = jnp.sum(exchange(up, COL).astype(F32), axis=0)
    u = upper.astype(BF)
    shifted = dot(u, cp)
    s = shifted.astype(BF)

    lp = dot(block, child).astype(BF).reshape(nc, rows, w)
    anc, x = ancestors(exchange(lp, COL), shifted, u.T, s.T, nr)
    x = exchange(x, ROW)
    t, r = slices(x, parent, child, cp)
    t = exchange(t, ROW)
    f = jnp.sum(exchange(rows_of(t, r, nc), COL), axis=0)

    pp_out = diag_upper + f[:own, :w]
    pc = f[own:, :w] - dot(pp_out.astype(BF), cp)
    cc = diag_lower + jnp.concatenate([f[:own, w:], f[own:, w:]], axis=1)
    return -upper, pp_out, anc, pc, cc


def solution(mesh):
    fine = Mesh(mesh.devices.reshape(4, 4, 2, 4, 2), ALL)
    out = P(ALL, None)
    return jax.shard_map(
        shards,
        mesh=fine,
        in_specs=(P(ROW, COL, None), out, P(), out, P(), P()),
        out_specs=(out,) * 5,
        check_vma=False,
    )
```

```python
import jax
import jax.numpy as jnp
from jax import lax
from jax.experimental import pallas as pl
from jax.experimental.pallas import tpu as pltpu
from jax.sharding import Mesh, PartitionSpec as P

ROW = ("x", "zh", "core")
COL = ("y", "zl")
ALL = ROW + COL
BF = jnp.bfloat16
F32 = jnp.float32
RING = (0, 1, 3, 2)


def dot(a, b, ca=1, cb=0):
    return lax.dot_general(a, b, (((ca,), (cb,)), ((), ())), preferred_element_type=F32)


def hold(a):
    return lax.optimization_barrier(a)


def exchange(a, axes):
    return lax.all_to_all(a, axes, 0, 0, tiled=True)


def shift(a, axis, by):
    n = lax.axis_size(axis)
    return lax.ppermute(a, axis, [(i, (i + by) % n) for i in range(n)])


def swap(a):
    return shift(a, "core", 1)


def ring(a, axis):
    return [a, shift(a, axis, -1), shift(a, axis, 1), shift(a, axis, 2)]


def lay_out(where, mine, others, panel, sems, blocks=range(4)):
    for n in blocks:
        for pieces, core in ((mine, where[2]), (others, 1 - where[2])):
            rows = pieces[0].shape[0] // 4
            for m, dz in enumerate(RING):
                piece, start = (pieces[n], m) if n < 3 else (pieces[3 + m // 2], m % 2)
                at = lax.rem(where[0] + RING[n], 4) * 4 + lax.rem(where[1] + dz, 4)
                at = pl.multiple_of((at * 2 + core) * rows, 32)
                pltpu.make_async_copy(
                    piece.at[pl.ds(start * rows, rows)], panel.at[pl.ds(at, rows)], sems.at[n]
                ).start()


def ring_block(n, where):
    return lax.rem(where[0] + RING[n], 4)


def near_kernel(where, *refs):
    z, out, panel, zcols, acc, sems, zsems, out_sem = refs[6:]
    depth = panel.shape[0] // 4

    def block(n):
        return pl.ds(pl.multiple_of(ring_block(n, where) * depth, 256), depth)

    zcopies = [pltpu.make_async_copy(z.at[:, block(n)], zcols.at[n], zsems.at[n]) for n in range(3)]
    for copy in zcopies:
        copy.start()
    lay_out(where, refs[:3], refs[3:6], panel, sems, range(3))
    for n in range(3):
        part = panel.at[block(n)]
        zcopies[n].wait()
        pltpu.make_async_copy(part, part, sems.at[n]).wait()
        got = jnp.dot(zcols[n], part[...], preferred_element_type=F32)
        if n == 0:
            acc[...] = got
        else:
            acc[...] += got
    copy = pltpu.make_async_copy(acc, out, out_sem)
    copy.start()
    copy.wait()


def far_kernel(where, *refs):
    near, z, out, panel, zcols, acc, result, sem, zsem, near_sem, out_sem = refs[4:]
    depth, rows = panel.shape[0], refs[0].shape[0] // 2
    at = ring_block(3, where)
    zcopy = pltpu.make_async_copy(
        z.at[:, pl.ds(pl.multiple_of(at * depth, 256), depth)], zcols, zsem
    )
    zcopy.start()
    for pieces, core in ((refs[:2], where[2]), (refs[2:4], 1 - where[2])):
        for m, dz in enumerate(RING):
            to = pl.multiple_of((lax.rem(where[1] + dz, 4) * 2 + core) * rows, 32)
            pltpu.make_async_copy(
                pieces[m // 2].at[pl.ds(m % 2 * rows, rows)], panel.at[pl.ds(to, rows)], sem
            ).start()
    ncopy = pltpu.make_async_copy(near, acc, near_sem)
    ncopy.start()
    zcopy.wait()
    pltpu.make_async_copy(panel, panel, sem).wait()
    got = jnp.dot(zcols[...], panel[...], preferred_element_type=F32)
    ncopy.wait()
    result[...] = (acc[...] + got).astype(BF).reshape(result.shape)
    copy = pltpu.make_async_copy(result, out, out_sem)
    copy.start()
    copy.wait()


def near_product(where, mine, others, z):
    depth, width = z.shape[1], mine[0].shape[1]
    hbm = pl.BlockSpec(memory_space=pltpu.HBM)
    return pl.pallas_call(
        near_kernel,
        grid_spec=pltpu.PrefetchScalarGridSpec(
            num_scalar_prefetch=1,
            grid=(),
            in_specs=[hbm] * 7,
            out_specs=hbm,
            scratch_shapes=[
                pltpu.VMEM((depth, width), BF),
                pltpu.VMEM((3, z.shape[0], depth // 4), BF),
                pltpu.VMEM((z.shape[0], width), F32),
                pltpu.SemaphoreType.DMA((3,)),
                pltpu.SemaphoreType.DMA((3,)),
                pltpu.SemaphoreType.DMA(()),
            ],
        ),
        out_shape=jax.ShapeDtypeStruct((z.shape[0], width), F32),
        compiler_params=pltpu.CompilerParams(vmem_limit_bytes=60 << 20),
        cost_estimate=pl.CostEstimate(
            flops=3 * z.size * width // 2,
            transcendentals=0,
            bytes_accessed=3 * z.size // 2 + 3 * depth * width // 2 + 4 * z.shape[0] * width,
        ),
    )(where, *mine, *others, z)


def far_product(where, mine, others, near, z, rows):
    depth, width = z.shape[1] // 4, near.shape[1]
    hbm = pl.BlockSpec(memory_space=pltpu.HBM)
    blocks = (z.shape[0] // rows, rows, width)
    return pl.pallas_call(
        far_kernel,
        grid_spec=pltpu.PrefetchScalarGridSpec(
            num_scalar_prefetch=1,
            grid=(),
            in_specs=[hbm] * 6,
            out_specs=hbm,
            scratch_shapes=[
                pltpu.VMEM((depth, width), BF),
                pltpu.VMEM((z.shape[0], depth), BF),
                pltpu.VMEM((z.shape[0], width), F32),
                pltpu.VMEM(blocks, BF),
                pltpu.SemaphoreType.DMA(()),
                pltpu.SemaphoreType.DMA(()),
                pltpu.SemaphoreType.DMA(()),
                pltpu.SemaphoreType.DMA(()),
            ],
        ),
        out_shape=jax.ShapeDtypeStruct(blocks, BF),
        compiler_params=pltpu.CompilerParams(vmem_limit_bytes=60 << 20),
        cost_estimate=pl.CostEstimate(
            flops=z.size * width // 2,
            transcendentals=0,
            bytes_accessed=z.size // 2 + 2 * depth * width + 6 * z.shape[0] * width,
        ),
    )(where, *mine, *others, near, z)


def panel_kernel(where, *refs):
    out, panel, sems, out_sem = refs[10:]
    depth = panel.shape[0] // 4
    lay_out(where, refs[:5], refs[5:10], panel, sems)
    copies = []
    for step in range(4):
        at = pl.ds(pl.multiple_of(ring_block(step, where) * depth, 256), depth)
        pltpu.make_async_copy(panel.at[at], panel.at[at], sems.at[step]).wait()
        copies.append(pltpu.make_async_copy(panel.at[at], out.at[at], out_sem.at[step]))
        copies[-1].start()
    for copy in copies:
        copy.wait()


def whole_panel(where, mine, others, depth):
    width = mine[0].shape[1]
    hbm = pl.BlockSpec(memory_space=pltpu.HBM)
    return pl.pallas_call(
        panel_kernel,
        grid_spec=pltpu.PrefetchScalarGridSpec(
            num_scalar_prefetch=1,
            grid=(),
            in_specs=[hbm] * 10,
            out_specs=hbm,
            scratch_shapes=[
                pltpu.VMEM((depth, width), BF),
                pltpu.SemaphoreType.DMA((4,)),
                pltpu.SemaphoreType.DMA((4,)),
            ],
        ),
        out_shape=jax.ShapeDtypeStruct((depth, width), BF),
        compiler_params=pltpu.CompilerParams(vmem_limit_bytes=60 << 20),
        cost_estimate=pl.CostEstimate(flops=0, transcendentals=0, bytes_accessed=4 * depth * width),
    )(where, *mine, *others)


def slices_kernel(x, parent, child, cp, t, r, xt, pbuf, cbuf, cpbuf, big, psem, csem, cpsem):
    nr, kinds, sl, rows = x.shape
    depth, w = parent.shape
    parts = psem.shape[0]
    chunk = depth // parts
    copies = []
    for n in range(parts):
        at = pl.ds(n * chunk, chunk)
        copies.append((pltpu.make_async_copy(parent.at[at], pbuf.at[at], psem.at[n]), pltpu.make_async_copy(child.at[at], cbuf.at[at], csem.at[n])))
        for c in copies[-1]:
            c.start()
    ccopy = pltpu.make_async_copy(cp, cpbuf, cpsem)
    ccopy.start()
    for s in range(nr):
        xt[:, s * rows : (s + 1) * rows] = x[s].reshape(kinds * sl, rows)
    for n in range(parts):
        at = pl.ds(n * chunk, chunk)
        for c in copies[n]:
            c.wait()
        lhs = xt[:, n * chunk : (n + 1) * chunk]
        gp = jnp.dot(lhs[: 2 * sl], pbuf[at, :], preferred_element_type=F32)
        gc = jnp.dot(lhs, cbuf[at, :], preferred_element_type=F32)
        if n == 0:
            big[: 2 * sl] = gp
            big[2 * sl :] = gc
        else:
            big[: 2 * sl] += gp
            big[2 * sl :] += gc
    ccopy.wait()
    r[0] = big[2 * sl : 3 * sl]
    r[1] = big[3 * sl : 4 * sl]
    t2 = jnp.dot(big[sl : 2 * sl].astype(BF), cpbuf[...], preferred_element_type=F32) + big[4 * sl :]
    big[sl : 2 * sl] = t2
    lane = lax.broadcasted_iota(jnp.int32, (16, 128), 1) // sl
    for q in range(w // 128):
        for d in range(4):
            out = None
            for g in range(4):
                v = big[g * 16 : (g + 1) * 16, q * 128 : (q + 1) * 128]
                v = pltpu.roll(v, ((g - d) * sl) % 128, 1) if g != d else v
                out = v if out is None else jnp.where(lane == g, v, out)
            t[q * 4 + d] = out

def slices(x, parent, child, cp):
    nr, kinds, sl, rows = x.shape
    depth, w = parent.shape
    parts = 4
    any_ = pl.BlockSpec(memory_space=pl.ANY)
    vm = pl.BlockSpec(memory_space=pltpu.VMEM)
    return pl.pallas_call(
        slices_kernel,
        in_specs=[vm, any_, any_, any_],
        out_specs=[vm, vm],
        out_shape=[jax.ShapeDtypeStruct((nr, 16, 128), F32), jax.ShapeDtypeStruct((2, sl, w), F32)],
        scratch_shapes=[pltpu.VMEM((kinds * sl, depth), BF), pltpu.VMEM((depth, w), BF), pltpu.VMEM((depth, w), BF), pltpu.VMEM(cp.shape, BF), pltpu.VMEM((5 * sl, w), F32),
            pltpu.SemaphoreType.DMA((parts,)), pltpu.SemaphoreType.DMA((parts,)), pltpu.SemaphoreType.DMA(())],
        compiler_params=pltpu.CompilerParams(vmem_limit_bytes=60 << 20),
        cost_estimate=pl.CostEstimate(flops=10 * sl * depth * w, transcendentals=0, bytes_accessed=4 * depth * w),
    )(x, parent, child, cp)

def rows_kernel(t, r, f, both):
    nr = t.shape[0]
    sl = r.shape[1]
    w = r.shape[2]
    for q in range(nr // 4):
        for kind in range(2):
            tall = []
            for d in range(4):
                for h in range(2):
                    v = t[q * 4 + d]
                    g = kind * 2 + h
                    tall.append(pltpu.roll(v, (128 - g * sl) % 128, 1) if g else v)
            tall = jnp.concatenate(tall, axis=0)
            both[kind, :, q * 128 : (q + 1) * 128] = tall.T[:sl]
    nc = f.shape[0]
    own = sl // nc
    half = w // 2
    for c in range(nc):
        at = slice(c * own, (c + 1) * own)
        low = both[1, at, :] - r[1, at, :]
        f[c, :own, :w] = both[0, at, :]
        f[c, own:, :w] = r[0, at, :]
        f[c, :own, w:] = low[:, :half]
        f[c, own:, w:] = low[:, half:]

def rows_of(t, r, nc):
    sl, w = r.shape[1:]
    vm = pl.BlockSpec(memory_space=pltpu.VMEM)
    return pl.pallas_call(
        rows_kernel, in_specs=[vm, vm], out_specs=vm,
        out_shape=jax.ShapeDtypeStruct((nc, 2 * sl // nc, 3 * w // 2), F32),
        scratch_shapes=[pltpu.VMEM((2, sl, w), F32)],
        compiler_params=pltpu.CompilerParams(vmem_limit_bytes=16 << 20),
        cost_estimate=pl.CostEstimate(flops=0, transcendentals=0, bytes_accessed=20 * sl * w),
    )(t, r)


def ancestors_kernel(got, shifted, ut, st, anc, x):
    nr, _, sl, rows = x.shape
    low = got[0].astype(F32)
    for n in range(1, got.shape[0]):
        low += got[n].astype(F32)
    low -= shifted[...]
    anc[...] = -low
    x[:, 0] = ut[...].reshape(nr, sl, rows)
    x[:, 1] = st[...].reshape(nr, sl, rows)
    x[:, 2] = low.T.astype(BF).reshape(nr, sl, rows)


def ancestors(got, shifted, ut, st, nr):
    rows, w = shifted.shape
    vmem = pl.BlockSpec(memory_space=pltpu.VMEM)
    return pl.pallas_call(
        ancestors_kernel,
        in_specs=[vmem] * 4,
        out_specs=[vmem] * 2,
        out_shape=[
            jax.ShapeDtypeStruct((rows, w), F32),
            jax.ShapeDtypeStruct((nr, 3, w // nr, rows), BF),
        ],
        compiler_params=pltpu.CompilerParams(vmem_limit_bytes=16 << 20),
        cost_estimate=pl.CostEstimate(flops=9 * rows * w, transcendentals=0, bytes_accessed=40 * rows * w),
    )(got, shifted, ut, st)


def shards(z, pp, pdi, ca, cp, cdi):
    rows, w = pp.shape
    nr, nc = lax.axis_size(ROW), lax.axis_size(COL)
    sl = w // nr
    own = sl // nc
    where = jnp.stack([lax.axis_index(a) for a in ROW]).astype(jnp.int32)
    block = z.reshape(z.shape[0], -1)

    child = lax.all_gather(ca, ROW, axis=0, tiled=True)
    diag_prod = dot(pdi, cp).astype(BF)
    first = (lax.axis_index(ROW) * nc + lax.axis_index(COL)) * own
    cols = lambda m: lax.dynamic_slice_in_dim(m, first, own, 1)
    diag_upper = dot(cols(pdi), pdi, 0, 0)
    diag_lower = dot(cols(cdi), cdi, 0, 0) + dot(cols(diag_prod), diag_prod, 0, 0)

    here = jnp.concatenate(ring(pp, "zh"))
    here, diag_upper, diag_lower = hold((here, diag_upper, diag_lower))
    after, before, here_other = hold((shift(here, "x", -1), shift(here, "x", 1), swap(here)))
    half = here.shape[0] // 2
    pieces = [here, after, before, shift(after[:half], "x", -1), shift(before[half:], "x", 1)]
    others = [here_other, swap(after), swap(before)]
    near = near_product(where, pieces[:3], others, block)
    pieces[3], pieces[4], near = hold((pieces[3], pieces[4], near))
    others += [swap(pieces[3]), swap(pieces[4])]
    up = far_product(where, pieces[3:], others[3:], near, block, rows)
    upper = jnp.sum(exchange(up, COL).astype(F32), axis=0)
    u = upper.astype(BF)
    shifted = dot(u, cp)
    s = shifted.astype(BF)

    lp = dot(block, child).astype(BF).reshape(nc, rows, w)
    got = exchange(lp, COL)
    anc, x = ancestors(got, shifted, u.T, s.T, nr)
    others[0], x = hold((others[0], x))
    x = exchange(x, ROW)
    parent = whole_panel(where, pieces, others, block.shape[1])
    t, r = slices(x, parent, child, cp)
    t = exchange(t, ROW)
    f = jnp.sum(exchange(rows_of(t, r, nc), COL), axis=0)

    pp_out = diag_upper + f[:own, :w]
    pc = f[own:, :w] - dot(pp_out.astype(BF), cp)
    cc = diag_lower + jnp.concatenate([f[:own, w:], f[own:, w:]], axis=1)
    return -upper, pp_out, anc, pc, cc


def solution(mesh):
    fine = Mesh(mesh.devices.reshape(4, 4, 2, 4, 2), ALL)
    out = P(ALL, None)
    return jax.shard_map(
        shards,
        mesh=fine,
        in_specs=(P(ROW, COL, None), out, P(), out, P(), P()),
        out_specs=(out,) * 5,
        check_vma=False,
    )
```

```python
import jax
import jax.numpy as jnp
from jax import lax
from jax.experimental import pallas as pl
from jax.experimental.pallas import tpu as pltpu
from jax.sharding import Mesh, PartitionSpec as P

ROW = ("x", "zh", "core")
COL = ("y", "zl")
ALL = ROW + COL
BF = jnp.bfloat16
F32 = jnp.float32
RING = (0, 1, 3, 2)


def dot(a, b, ca=1, cb=0):
    return lax.dot_general(a, b, (((ca,), (cb,)), ((), ())), preferred_element_type=F32)


def hold(a):
    return lax.optimization_barrier(a)


def exchange(a, axes):
    return lax.all_to_all(a, axes, 0, 0, tiled=True)


def shift(a, axis, by):
    n = lax.axis_size(axis)
    return lax.ppermute(a, axis, [(i, (i + by) % n) for i in range(n)])


def swap(a):
    return shift(a, "core", 1)


def ring(a, axis):
    return [a, shift(a, axis, -1), shift(a, axis, 1), shift(a, axis, 2)]


def lay_out(where, mine, others, panel, sems, blocks=range(4)):
    for n in blocks:
        for pieces, core in ((mine, where[2]), (others, 1 - where[2])):
            rows = pieces[0].shape[0] // 4
            for m, dz in enumerate(RING):
                piece, start = (pieces[n], m) if n < 3 else (pieces[3 + m // 2], m % 2)
                at = lax.rem(where[0] + RING[n], 4) * 4 + lax.rem(where[1] + dz, 4)
                at = pl.multiple_of((at * 2 + core) * rows, 32)
                pltpu.make_async_copy(
                    piece.at[pl.ds(start * rows, rows)], panel.at[pl.ds(at, rows)], sems.at[n]
                ).start()


def ring_block(n, where):
    return lax.rem(where[0] + RING[n], 4)


def near_kernel(where, *refs):
    z, out, panel, zcols, acc, sems, zsems, out_sem = refs[6:]
    depth = panel.shape[0] // 4

    def block(n):
        return pl.ds(pl.multiple_of(ring_block(n, where) * depth, 256), depth)

    zcopies = [pltpu.make_async_copy(z.at[:, block(n)], zcols.at[n], zsems.at[n]) for n in range(3)]
    for copy in zcopies:
        copy.start()
    lay_out(where, refs[:3], refs[3:6], panel, sems, range(3))
    for n in range(3):
        part = panel.at[block(n)]
        zcopies[n].wait()
        pltpu.make_async_copy(part, part, sems.at[n]).wait()
        got = jnp.dot(zcols[n], part[...], preferred_element_type=F32)
        if n == 0:
            acc[...] = got
        else:
            acc[...] += got
    copy = pltpu.make_async_copy(acc, out, out_sem)
    copy.start()
    copy.wait()


def far_kernel(where, *refs):
    near, z, out, own, panel, zcols, acc, result, sem, zsem, near_sem, out_sem, own_sem = refs[4:]
    depth, rows = panel.shape[0], refs[0].shape[0] // 2
    at = ring_block(3, where)
    zcopy = pltpu.make_async_copy(
        z.at[:, pl.ds(pl.multiple_of(at * depth, 256), depth)], zcols, zsem
    )
    zcopy.start()
    for pieces, core in ((refs[:2], where[2]), (refs[2:4], 1 - where[2])):
        for m, dz in enumerate(RING):
            to = pl.multiple_of((lax.rem(where[1] + dz, 4) * 2 + core) * rows, 32)
            pltpu.make_async_copy(
                pieces[m // 2].at[pl.ds(m % 2 * rows, rows)], panel.at[pl.ds(to, rows)], sem
            ).start()
    ncopy = pltpu.make_async_copy(near, acc, near_sem)
    ncopy.start()
    zcopy.wait()
    pltpu.make_async_copy(panel, panel, sem).wait()
    got = jnp.dot(zcols[...], panel[...], preferred_element_type=F32)
    ncopy.wait()
    got += acc[...]
    acc[...] = got
    result[...] = got.astype(BF).reshape(result.shape)
    copy = pltpu.make_async_copy(result, out, out_sem)
    copy.start()
    at = pl.multiple_of(where[3] * rows, 32)
    keep = pltpu.make_async_copy(acc.at[pl.ds(at, rows)], own, own_sem)
    keep.start()
    copy.wait()
    keep.wait()


def near_product(where, mine, others, z):
    depth, width = z.shape[1], mine[0].shape[1]
    hbm = pl.BlockSpec(memory_space=pltpu.HBM)
    return pl.pallas_call(
        near_kernel,
        grid_spec=pltpu.PrefetchScalarGridSpec(
            num_scalar_prefetch=1,
            grid=(),
            in_specs=[hbm] * 7,
            out_specs=hbm,
            scratch_shapes=[
                pltpu.VMEM((depth, width), BF),
                pltpu.VMEM((3, z.shape[0], depth // 4), BF),
                pltpu.VMEM((z.shape[0], width), F32),
                pltpu.SemaphoreType.DMA((3,)),
                pltpu.SemaphoreType.DMA((3,)),
                pltpu.SemaphoreType.DMA(()),
            ],
        ),
        out_shape=jax.ShapeDtypeStruct((z.shape[0], width), F32),
        compiler_params=pltpu.CompilerParams(vmem_limit_bytes=60 << 20),
        cost_estimate=pl.CostEstimate(
            flops=3 * z.size * width // 2,
            transcendentals=0,
            bytes_accessed=3 * z.size // 2 + 3 * depth * width // 2 + 4 * z.shape[0] * width,
        ),
    )(where, *mine, *others, z)


def far_product(where, mine, others, near, z, rows):
    depth, width = z.shape[1] // 4, near.shape[1]
    hbm = pl.BlockSpec(memory_space=pltpu.HBM)
    blocks = (z.shape[0] // rows, rows, width)
    return pl.pallas_call(
        far_kernel,
        grid_spec=pltpu.PrefetchScalarGridSpec(
            num_scalar_prefetch=1,
            grid=(),
            in_specs=[hbm] * 6,
            out_specs=[hbm] * 2,
            scratch_shapes=[
                pltpu.VMEM((depth, width), BF),
                pltpu.VMEM((z.shape[0], depth), BF),
                pltpu.VMEM((z.shape[0], width), F32),
                pltpu.VMEM(blocks, BF),
                pltpu.SemaphoreType.DMA(()),
                pltpu.SemaphoreType.DMA(()),
                pltpu.SemaphoreType.DMA(()),
                pltpu.SemaphoreType.DMA(()),
                pltpu.SemaphoreType.DMA(()),
            ],
        ),
        out_shape=[jax.ShapeDtypeStruct(blocks, BF), jax.ShapeDtypeStruct((rows, width), F32)],
        compiler_params=pltpu.CompilerParams(vmem_limit_bytes=60 << 20),
        cost_estimate=pl.CostEstimate(
            flops=z.size * width // 2,
            transcendentals=0,
            bytes_accessed=z.size // 2 + 2 * depth * width + 6 * z.shape[0] * width,
        ),
    )(where, *mine, *others, near, z)


def panel_kernel(where, *refs):
    out, panel, sems, out_sem = refs[10:]
    depth = panel.shape[0] // 4
    lay_out(where, refs[:5], refs[5:10], panel, sems)
    copies = []
    for step in range(4):
        at = pl.ds(pl.multiple_of(ring_block(step, where) * depth, 256), depth)
        pltpu.make_async_copy(panel.at[at], panel.at[at], sems.at[step]).wait()
        copies.append(pltpu.make_async_copy(panel.at[at], out.at[at], out_sem.at[step]))
        copies[-1].start()
    for copy in copies:
        copy.wait()


def whole_panel(where, mine, others, depth):
    width = mine[0].shape[1]
    hbm = pl.BlockSpec(memory_space=pltpu.HBM)
    return pl.pallas_call(
        panel_kernel,
        grid_spec=pltpu.PrefetchScalarGridSpec(
            num_scalar_prefetch=1,
            grid=(),
            in_specs=[hbm] * 10,
            out_specs=hbm,
            scratch_shapes=[
                pltpu.VMEM((depth, width), BF),
                pltpu.SemaphoreType.DMA((4,)),
                pltpu.SemaphoreType.DMA((4,)),
            ],
        ),
        out_shape=jax.ShapeDtypeStruct((depth, width), BF),
        compiler_params=pltpu.CompilerParams(vmem_limit_bytes=60 << 20),
        cost_estimate=pl.CostEstimate(flops=0, transcendentals=0, bytes_accessed=4 * depth * width),
    )(where, *mine, *others)


def slices_kernel(x, parent, child, cp, t, r, xt, pbuf, cbuf, cpbuf, big, psem, csem, cpsem):
    nr, kinds, sl, rows = x.shape
    depth, w = parent.shape
    parts = psem.shape[0]
    chunk = depth // parts
    copies = []
    for n in range(parts):
        at = pl.ds(n * chunk, chunk)
        copies.append((pltpu.make_async_copy(parent.at[at], pbuf.at[at], psem.at[n]), pltpu.make_async_copy(child.at[at], cbuf.at[at], csem.at[n])))
        for c in copies[-1]:
            c.start()
    ccopy = pltpu.make_async_copy(cp, cpbuf, cpsem)
    ccopy.start()
    for s in range(nr):
        xt[:, s * rows : (s + 1) * rows] = x[s].reshape(kinds * sl, rows)
    for n in range(parts):
        at = pl.ds(n * chunk, chunk)
        for c in copies[n]:
            c.wait()
        lhs = xt[:, n * chunk : (n + 1) * chunk]
        gp = jnp.dot(lhs[: 2 * sl], pbuf[at, :], preferred_element_type=F32)
        gc = jnp.dot(lhs, cbuf[at, :], preferred_element_type=F32)
        if n == 0:
            big[: 2 * sl] = gp
            big[2 * sl :] = gc
        else:
            big[: 2 * sl] += gp
            big[2 * sl :] += gc
    ccopy.wait()
    r[0] = big[2 * sl : 3 * sl]
    r[1] = big[3 * sl : 4 * sl]
    t2 = jnp.dot(big[sl : 2 * sl].astype(BF), cpbuf[...], preferred_element_type=F32) + big[4 * sl :]
    big[sl : 2 * sl] = t2
    lane = lax.broadcasted_iota(jnp.int32, (16, 128), 1) // sl
    for q in range(w // 128):
        for d in range(4):
            out = None
            for g in range(4):
                v = big[g * 16 : (g + 1) * 16, q * 128 : (q + 1) * 128]
                v = pltpu.roll(v, ((g - d) * sl) % 128, 1) if g != d else v
                out = v if out is None else jnp.where(lane == g, v, out)
            t[q * 4 + d] = out.astype(BF)

def slices(x, parent, child, cp):
    nr, kinds, sl, rows = x.shape
    depth, w = parent.shape
    parts = 4
    any_ = pl.BlockSpec(memory_space=pl.ANY)
    vm = pl.BlockSpec(memory_space=pltpu.VMEM)
    return pl.pallas_call(
        slices_kernel,
        in_specs=[vm, any_, any_, any_],
        out_specs=[vm, vm],
        out_shape=[jax.ShapeDtypeStruct((nr, 16, 128), BF), jax.ShapeDtypeStruct((2, sl, w), F32)],
        scratch_shapes=[pltpu.VMEM((kinds * sl, depth), BF), pltpu.VMEM((depth, w), BF), pltpu.VMEM((depth, w), BF), pltpu.VMEM(cp.shape, BF), pltpu.VMEM((5 * sl, w), F32),
            pltpu.SemaphoreType.DMA((parts,)), pltpu.SemaphoreType.DMA((parts,)), pltpu.SemaphoreType.DMA(())],
        compiler_params=pltpu.CompilerParams(vmem_limit_bytes=60 << 20),
        cost_estimate=pl.CostEstimate(flops=10 * sl * depth * w, transcendentals=0, bytes_accessed=4 * depth * w),
    )(x, parent, child, cp)

def rows_kernel(t, r, f, both):
    nr = t.shape[0]
    sl = r.shape[1]
    w = r.shape[2]
    for q in range(nr // 4):
        for kind in range(2):
            tall = []
            for d in range(4):
                for h in range(2):
                    v = t[q * 4 + d].astype(F32)
                    g = kind * 2 + h
                    tall.append(pltpu.roll(v, (128 - g * sl) % 128, 1) if g else v)
            tall = jnp.concatenate(tall, axis=0)
            both[kind, :, q * 128 : (q + 1) * 128] = tall.T[:sl]
    nc = f.shape[0]
    own = sl // nc
    half = w // 2
    for c in range(nc):
        at = slice(c * own, (c + 1) * own)
        low = both[1, at, :] - r[1, at, :]
        f[c, :own, :w] = both[0, at, :]
        f[c, own:, :w] = r[0, at, :]
        f[c, :own, w:] = low[:, :half]
        f[c, own:, w:] = low[:, half:]

def rows_of(t, r, nc):
    sl, w = r.shape[1:]
    vm = pl.BlockSpec(memory_space=pltpu.VMEM)
    return pl.pallas_call(
        rows_kernel, in_specs=[vm, vm], out_specs=vm,
        out_shape=jax.ShapeDtypeStruct((nc, 2 * sl // nc, 3 * w // 2), F32),
        scratch_shapes=[pltpu.VMEM((2, sl, w), F32)],
        compiler_params=pltpu.CompilerParams(vmem_limit_bytes=16 << 20),
        cost_estimate=pl.CostEstimate(flops=0, transcendentals=0, bytes_accessed=20 * sl * w),
    )(t, r)


def ancestors_kernel(where, got, own, shifted, ut, st, anc, x):
    nr, _, sl, rows = x.shape
    low = own[...] - shifted[...]
    for n in range(got.shape[0]):
        low += jnp.where(where[3] == n, 0.0, got[n].astype(F32))
    anc[...] = -low
    x[:, 0] = ut[...].reshape(nr, sl, rows)
    x[:, 1] = st[...].reshape(nr, sl, rows)
    x[:, 2] = low.T.astype(BF).reshape(nr, sl, rows)


def ancestors(where, got, own, shifted, ut, st, nr):
    rows, w = shifted.shape
    vmem = pl.BlockSpec(memory_space=pltpu.VMEM)
    return pl.pallas_call(
        ancestors_kernel,
        in_specs=[pl.BlockSpec(memory_space=pltpu.SMEM)] + [vmem] * 5,
        out_specs=[vmem] * 2,
        out_shape=[
            jax.ShapeDtypeStruct((rows, w), F32),
            jax.ShapeDtypeStruct((nr, 3, w // nr, rows), BF),
        ],
        compiler_params=pltpu.CompilerParams(vmem_limit_bytes=16 << 20),
        cost_estimate=pl.CostEstimate(flops=9 * rows * w, transcendentals=0, bytes_accessed=40 * rows * w),
    )(where, got, own, shifted, ut, st)


def shards(z, pp, pdi, ca, cp, cdi):
    rows, w = pp.shape
    nr, nc = lax.axis_size(ROW), lax.axis_size(COL)
    sl = w // nr
    own = sl // nc
    where = jnp.stack([lax.axis_index(a) for a in ROW + (COL,)]).astype(jnp.int32)
    block = z.reshape(z.shape[0], -1)

    child = lax.all_gather(ca, ROW, axis=0, tiled=True)
    diag_prod = dot(pdi, cp).astype(BF)
    first = (lax.axis_index(ROW) * nc + lax.axis_index(COL)) * own
    cols = lambda m: lax.dynamic_slice_in_dim(m, first, own, 1)
    diag_upper = dot(cols(pdi), pdi, 0, 0)
    diag_lower = dot(cols(cdi), cdi, 0, 0) + dot(cols(diag_prod), diag_prod, 0, 0)

    here = jnp.concatenate(ring(pp, "zh"))
    here, diag_upper, diag_lower = hold((here, diag_upper, diag_lower))
    after, before, here_other = hold((shift(here, "x", -1), shift(here, "x", 1), swap(here)))
    half = here.shape[0] // 2
    pieces = [here, after, before, shift(after[:half], "x", -1), shift(before[half:], "x", 1)]
    others = [here_other, swap(after), swap(before)]
    near = near_product(where, pieces[:3], others, block)
    pieces[3], pieces[4], near = hold((pieces[3], pieces[4], near))
    others += [swap(pieces[3]), swap(pieces[4])]
    up, own_up = far_product(where, pieces[3:], others[3:], near, block, rows)
    foreign = (jnp.arange(nc) != where[3])[:, None, None]
    upper = own_up + jnp.sum(jnp.where(foreign, exchange(up, COL).astype(F32), 0.0), axis=0)
    u = upper.astype(BF)
    shifted = dot(u, cp)
    s = shifted.astype(BF)

    lp = dot(block, child).astype(BF).reshape(nc, rows, w)
    got = exchange(lp, COL)
    own_lp = dot(lax.dynamic_slice_in_dim(block, where[3] * rows, rows, 0), child)
    anc, x = ancestors(where, got, own_lp, shifted, u.T, s.T, nr)
    others[0], x = hold((others[0], x))
    x = exchange(x, ROW)
    parent = whole_panel(where, pieces, others, block.shape[1])
    t, r = slices(x, parent, child, cp)
    t = exchange(t, ROW)
    f = jnp.sum(exchange(rows_of(t, r, nc), COL), axis=0)

    pp_out = diag_upper + f[:own, :w]
    pc = f[own:, :w] - dot(pp_out.astype(BF), cp)
    cc = diag_lower + jnp.concatenate([f[:own, w:], f[own:, w:]], axis=1)
    return -upper, pp_out, anc, pc, cc


def solution(mesh):
    fine = Mesh(mesh.devices.reshape(4, 4, 2, 4, 2), ALL)
    out = P(ALL, None)
    return jax.shard_map(
        shards,
        mesh=fine,
        in_specs=(P(ROW, COL, None), out, P(), out, P(), P()),
        out_specs=(out,) * 5,
        check_vma=False,
    )
```

```python
import jax
import jax.numpy as jnp
from jax import lax
from jax.experimental import pallas as pl
from jax.experimental.pallas import tpu as pltpu
from jax.sharding import Mesh, PartitionSpec as P

ROW = ("x", "zh", "core")
COL = ("y", "zl")
ALL = ROW + COL
BF = jnp.bfloat16
F32 = jnp.float32
RING = (0, 1, 3, 2)


def dot(a, b, ca=1, cb=0):
    return lax.dot_general(a, b, (((ca,), (cb,)), ((), ())), preferred_element_type=F32)


def hold(a):
    return lax.optimization_barrier(a)


def exchange(a, axes):
    return lax.all_to_all(a, axes, 0, 0, tiled=True)


def shift(a, axis, by):
    n = lax.axis_size(axis)
    return lax.ppermute(a, axis, [(i, (i + by) % n) for i in range(n)])


def swap(a):
    return shift(a, "core", 1)


def ring(a, axis):
    return [a, shift(a, axis, -1), shift(a, axis, 1), shift(a, axis, 2)]


def lay_out(where, mine, others, panel, sems, blocks=range(4)):
    for n in blocks:
        for pieces, core in ((mine, where[2]), (others, 1 - where[2])):
            rows = pieces[0].shape[0] // 4
            for m, dz in enumerate(RING):
                piece, start = (pieces[n], m) if n < 3 else (pieces[3 + m // 2], m % 2)
                at = lax.rem(where[0] + RING[n], 4) * 4 + lax.rem(where[1] + dz, 4)
                at = pl.multiple_of((at * 2 + core) * rows, 32)
                pltpu.make_async_copy(
                    piece.at[pl.ds(start * rows, rows)], panel.at[pl.ds(at, rows)], sems.at[n]
                ).start()


def ring_block(n, where):
    return lax.rem(where[0] + RING[n], 4)


def near_kernel(where, *refs):
    z, out, panel, zcols, acc, sems, zsems, out_sem = refs[6:]
    depth = panel.shape[0] // 4

    def block(n):
        return pl.ds(pl.multiple_of(ring_block(n, where) * depth, 256), depth)

    zcopies = [pltpu.make_async_copy(z.at[:, block(n)], zcols.at[n], zsems.at[n]) for n in range(3)]
    for copy in zcopies:
        copy.start()
    lay_out(where, refs[:3], refs[3:6], panel, sems, range(3))
    for n in range(3):
        part = panel.at[block(n)]
        zcopies[n].wait()
        pltpu.make_async_copy(part, part, sems.at[n]).wait()
        got = jnp.dot(zcols[n], part[...], preferred_element_type=F32)
        if n == 0:
            acc[...] = got
        else:
            acc[...] += got
    copy = pltpu.make_async_copy(acc, out, out_sem)
    copy.start()
    copy.wait()


def far_kernel(where, *refs):
    near, z, out, own, panel, zcols, acc, result, sem, zsem, near_sem, out_sem, own_sem = refs[4:]
    depth, rows = panel.shape[0], refs[0].shape[0] // 2
    at = ring_block(3, where)
    zcopy = pltpu.make_async_copy(
        z.at[:, pl.ds(pl.multiple_of(at * depth, 256), depth)], zcols, zsem
    )
    zcopy.start()
    for pieces, core in ((refs[:2], where[2]), (refs[2:4], 1 - where[2])):
        for m, dz in enumerate(RING):
            to = pl.multiple_of((lax.rem(where[1] + dz, 4) * 2 + core) * rows, 32)
            pltpu.make_async_copy(
                pieces[m // 2].at[pl.ds(m % 2 * rows, rows)], panel.at[pl.ds(to, rows)], sem
            ).start()
    ncopy = pltpu.make_async_copy(near, acc, near_sem)
    ncopy.start()
    zcopy.wait()
    pltpu.make_async_copy(panel, panel, sem).wait()
    got = jnp.dot(zcols[...], panel[...], preferred_element_type=F32)
    ncopy.wait()
    got += acc[...]
    acc[...] = got
    result[...] = got.astype(BF).reshape(result.shape)
    copy = pltpu.make_async_copy(result, out, out_sem)
    copy.start()
    at = pl.multiple_of(where[3] * rows, 32)
    keep = pltpu.make_async_copy(acc.at[pl.ds(at, rows)], own, own_sem)
    keep.start()
    copy.wait()
    keep.wait()


def near_product(where, mine, others, z):
    depth, width = z.shape[1], mine[0].shape[1]
    hbm = pl.BlockSpec(memory_space=pltpu.HBM)
    return pl.pallas_call(
        near_kernel,
        grid_spec=pltpu.PrefetchScalarGridSpec(
            num_scalar_prefetch=1,
            grid=(),
            in_specs=[hbm] * 7,
            out_specs=hbm,
            scratch_shapes=[
                pltpu.VMEM((depth, width), BF),
                pltpu.VMEM((3, z.shape[0], depth // 4), BF),
                pltpu.VMEM((z.shape[0], width), F32),
                pltpu.SemaphoreType.DMA((3,)),
                pltpu.SemaphoreType.DMA((3,)),
                pltpu.SemaphoreType.DMA(()),
            ],
        ),
        out_shape=jax.ShapeDtypeStruct((z.shape[0], width), F32),
        compiler_params=pltpu.CompilerParams(vmem_limit_bytes=24 << 20),
        cost_estimate=pl.CostEstimate(
            flops=3 * z.size * width // 2,
            transcendentals=0,
            bytes_accessed=3 * z.size // 2 + 3 * depth * width // 2 + 4 * z.shape[0] * width,
        ),
    )(where, *mine, *others, z)


def far_product(where, mine, others, near, z, rows):
    depth, width = z.shape[1] // 4, near.shape[1]
    hbm = pl.BlockSpec(memory_space=pltpu.HBM)
    blocks = (z.shape[0] // rows, rows, width)
    return pl.pallas_call(
        far_kernel,
        grid_spec=pltpu.PrefetchScalarGridSpec(
            num_scalar_prefetch=1,
            grid=(),
            in_specs=[hbm] * 6,
            out_specs=[hbm] * 2,
            scratch_shapes=[
                pltpu.VMEM((depth, width), BF),
                pltpu.VMEM((z.shape[0], depth), BF),
                pltpu.VMEM((z.shape[0], width), F32),
                pltpu.VMEM(blocks, BF),
                pltpu.SemaphoreType.DMA(()),
                pltpu.SemaphoreType.DMA(()),
                pltpu.SemaphoreType.DMA(()),
                pltpu.SemaphoreType.DMA(()),
                pltpu.SemaphoreType.DMA(()),
            ],
        ),
        out_shape=[jax.ShapeDtypeStruct(blocks, BF), jax.ShapeDtypeStruct((rows, width), F32)],
        compiler_params=pltpu.CompilerParams(vmem_limit_bytes=24 << 20),
        cost_estimate=pl.CostEstimate(
            flops=z.size * width // 2,
            transcendentals=0,
            bytes_accessed=z.size // 2 + 2 * depth * width + 6 * z.shape[0] * width,
        ),
    )(where, *mine, *others, near, z)


def panel_kernel(where, *refs):
    out, panel, sems, out_sem = refs[10:]
    depth = panel.shape[0] // 4
    lay_out(where, refs[:5], refs[5:10], panel, sems)
    copies = []
    for step in range(4):
        at = pl.ds(pl.multiple_of(ring_block(step, where) * depth, 256), depth)
        pltpu.make_async_copy(panel.at[at], panel.at[at], sems.at[step]).wait()
        copies.append(pltpu.make_async_copy(panel.at[at], out.at[at], out_sem.at[step]))
        copies[-1].start()
    for copy in copies:
        copy.wait()


def whole_panel(where, mine, others, depth):
    width = mine[0].shape[1]
    hbm = pl.BlockSpec(memory_space=pltpu.HBM)
    return pl.pallas_call(
        panel_kernel,
        grid_spec=pltpu.PrefetchScalarGridSpec(
            num_scalar_prefetch=1,
            grid=(),
            in_specs=[hbm] * 10,
            out_specs=hbm,
            scratch_shapes=[
                pltpu.VMEM((depth, width), BF),
                pltpu.SemaphoreType.DMA((4,)),
                pltpu.SemaphoreType.DMA((4,)),
            ],
        ),
        out_shape=jax.ShapeDtypeStruct((depth, width), BF),
        compiler_params=pltpu.CompilerParams(vmem_limit_bytes=60 << 20),
        cost_estimate=pl.CostEstimate(flops=0, transcendentals=0, bytes_accessed=4 * depth * width),
    )(where, *mine, *others)


def slices_kernel(x, parent, child, cp, t, r, xt, pbuf, cbuf, cpbuf, big, psem, csem, cpsem):
    nr, kinds, sl, rows = x.shape
    depth, w = parent.shape
    parts = psem.shape[0]
    chunk = depth // parts
    copies = []
    for n in range(parts):
        at = pl.ds(n * chunk, chunk)
        copies.append((pltpu.make_async_copy(parent.at[at], pbuf.at[at], psem.at[n]), pltpu.make_async_copy(child.at[at], cbuf.at[at], csem.at[n])))
        for c in copies[-1]:
            c.start()
    ccopy = pltpu.make_async_copy(cp, cpbuf, cpsem)
    ccopy.start()
    for s in range(nr):
        xt[:, s * rows : (s + 1) * rows] = x[s].reshape(kinds * sl, rows)
    for n in range(parts):
        at = pl.ds(n * chunk, chunk)
        for c in copies[n]:
            c.wait()
        lhs = xt[:, n * chunk : (n + 1) * chunk]
        gp = jnp.dot(lhs[: 2 * sl], pbuf[at, :], preferred_element_type=F32)
        gc = jnp.dot(lhs, cbuf[at, :], preferred_element_type=F32)
        if n == 0:
            big[: 2 * sl] = gp
            big[2 * sl :] = gc
        else:
            big[: 2 * sl] += gp
            big[2 * sl :] += gc
    ccopy.wait()
    r[0] = big[2 * sl : 3 * sl]
    r[1] = big[3 * sl : 4 * sl]
    t2 = jnp.dot(big[sl : 2 * sl].astype(BF), cpbuf[...], preferred_element_type=F32) + big[4 * sl :]
    big[sl : 2 * sl] = t2
    lane = lax.broadcasted_iota(jnp.int32, (16, 128), 1) // sl
    for q in range(w // 128):
        for d in range(4):
            out = None
            for g in range(4):
                v = big[g * 16 : (g + 1) * 16, q * 128 : (q + 1) * 128]
                v = pltpu.roll(v, ((g - d) * sl) % 128, 1) if g != d else v
                out = v if out is None else jnp.where(lane == g, v, out)
            t[q * 4 + d] = out.astype(BF)

def slices(x, parent, child, cp):
    nr, kinds, sl, rows = x.shape
    depth, w = parent.shape
    parts = 4
    any_ = pl.BlockSpec(memory_space=pl.ANY)
    vm = pl.BlockSpec(memory_space=pltpu.VMEM)
    return pl.pallas_call(
        slices_kernel,
        in_specs=[vm, any_, any_, any_],
        out_specs=[vm, vm],
        out_shape=[jax.ShapeDtypeStruct((nr, 16, 128), BF), jax.ShapeDtypeStruct((2, sl, w), F32)],
        scratch_shapes=[pltpu.VMEM((kinds * sl, depth), BF), pltpu.VMEM((depth, w), BF), pltpu.VMEM((depth, w), BF), pltpu.VMEM(cp.shape, BF), pltpu.VMEM((5 * sl, w), F32),
            pltpu.SemaphoreType.DMA((parts,)), pltpu.SemaphoreType.DMA((parts,)), pltpu.SemaphoreType.DMA(())],
        compiler_params=pltpu.CompilerParams(vmem_limit_bytes=60 << 20),
        cost_estimate=pl.CostEstimate(flops=10 * sl * depth * w, transcendentals=0, bytes_accessed=4 * depth * w),
    )(x, parent, child, cp)

def rows_kernel(t, r, f, both):
    nr = t.shape[0]
    sl = r.shape[1]
    w = r.shape[2]
    for q in range(nr // 4):
        for kind in range(2):
            tall = []
            for d in range(4):
                for h in range(2):
                    v = t[q * 4 + d].astype(F32)
                    g = kind * 2 + h
                    tall.append(pltpu.roll(v, (128 - g * sl) % 128, 1) if g else v)
            tall = jnp.concatenate(tall, axis=0)
            both[kind, :, q * 128 : (q + 1) * 128] = tall.T[:sl]
    nc = f.shape[0]
    own = sl // nc
    half = w // 2
    for c in range(nc):
        at = slice(c * own, (c + 1) * own)
        low = both[1, at, :] - r[1, at, :]
        f[c, :own, :w] = both[0, at, :]
        f[c, own:, :w] = r[0, at, :]
        f[c, :own, w:] = low[:, :half]
        f[c, own:, w:] = low[:, half:]

def rows_of(t, r, nc):
    sl, w = r.shape[1:]
    vm = pl.BlockSpec(memory_space=pltpu.VMEM)
    return pl.pallas_call(
        rows_kernel, in_specs=[vm, vm], out_specs=vm,
        out_shape=jax.ShapeDtypeStruct((nc, 2 * sl // nc, 3 * w // 2), F32),
        scratch_shapes=[pltpu.VMEM((2, sl, w), F32)],
        compiler_params=pltpu.CompilerParams(vmem_limit_bytes=16 << 20),
        cost_estimate=pl.CostEstimate(flops=0, transcendentals=0, bytes_accessed=20 * sl * w),
    )(t, r)


def ancestors_kernel(where, got, own, shifted, ut, st, anc, x):
    nr, _, sl, rows = x.shape
    low = own[...] - shifted[...]
    for n in range(got.shape[0]):
        low += jnp.where(where[3] == n, 0.0, got[n].astype(F32))
    anc[...] = -low
    x[:, 0] = ut[...].reshape(nr, sl, rows)
    x[:, 1] = st[...].reshape(nr, sl, rows)
    x[:, 2] = low.T.astype(BF).reshape(nr, sl, rows)


def ancestors(where, got, own, shifted, ut, st, nr):
    rows, w = shifted.shape
    vmem = pl.BlockSpec(memory_space=pltpu.VMEM)
    return pl.pallas_call(
        ancestors_kernel,
        in_specs=[pl.BlockSpec(memory_space=pltpu.SMEM)] + [vmem] * 5,
        out_specs=[vmem] * 2,
        out_shape=[
            jax.ShapeDtypeStruct((rows, w), F32),
            jax.ShapeDtypeStruct((nr, 3, w // nr, rows), BF),
        ],
        compiler_params=pltpu.CompilerParams(vmem_limit_bytes=16 << 20),
        cost_estimate=pl.CostEstimate(flops=9 * rows * w, transcendentals=0, bytes_accessed=40 * rows * w),
    )(where, got, own, shifted, ut, st)


def shards(z, pp, pdi, ca, cp, cdi):
    rows, w = pp.shape
    nr, nc = lax.axis_size(ROW), lax.axis_size(COL)
    sl = w // nr
    own = sl // nc
    where = jnp.stack([lax.axis_index(a) for a in ROW + (COL,)]).astype(jnp.int32)
    block = z.reshape(z.shape[0], -1)

    child = lax.all_gather(ca, ROW, axis=0, tiled=True)
    diag_prod = dot(pdi, cp).astype(BF)
    first = (lax.axis_index(ROW) * nc + lax.axis_index(COL)) * own
    cols = lambda m: lax.dynamic_slice_in_dim(m, first, own, 1)
    diag_upper = dot(cols(pdi), pdi, 0, 0)
    diag_lower = dot(cols(cdi), cdi, 0, 0) + dot(cols(diag_prod), diag_prod, 0, 0)

    here = jnp.concatenate(ring(pp, "zh"))
    here, diag_upper, diag_lower = hold((here, diag_upper, diag_lower))
    after, before, here_other = hold((shift(here, "x", -1), shift(here, "x", 1), swap(here)))
    half = here.shape[0] // 2
    pieces = [here, after, before, shift(after[:half], "x", -1), shift(before[half:], "x", 1)]
    others = [here_other, swap(after), swap(before)]
    near = near_product(where, pieces[:3], others, block)
    pieces[3], pieces[4], near = hold((pieces[3], pieces[4], near))
    others += [swap(pieces[3]), swap(pieces[4])]
    up, own_up = far_product(where, pieces[3:], others[3:], near, block, rows)
    foreign = (jnp.arange(nc) != where[3])[:, None, None]
    upper = own_up + jnp.sum(jnp.where(foreign, exchange(up, COL).astype(F32), 0.0), axis=0)
    u = upper.astype(BF)
    shifted = dot(u, cp)
    s = shifted.astype(BF)

    lp = dot(block, child).astype(BF).reshape(nc, rows, w)
    got = exchange(lp, COL)
    own_lp = dot(lax.dynamic_slice_in_dim(block, where[3] * rows, rows, 0), child)
    anc, x = ancestors(where, got, own_lp, shifted, u.T, s.T, nr)
    others[0], x = hold((others[0], x))
    x = exchange(x, ROW)
    parent = whole_panel(where, pieces, others, block.shape[1])
    t, r = slices(x, parent, child, cp)
    t = exchange(t, ROW)
    f = jnp.sum(exchange(rows_of(t, r, nc), COL), axis=0)

    pp_out = diag_upper + f[:own, :w]
    pc = f[own:, :w] - dot(pp_out.astype(BF), cp)
    cc = diag_lower + jnp.concatenate([f[:own, w:], f[own:, w:]], axis=1)
    return -upper, pp_out, anc, pc, cc


def solution(mesh):
    fine = Mesh(mesh.devices.reshape(4, 4, 2, 4, 2), ALL)
    out = P(ALL, None)
    return jax.shard_map(
        shards,
        mesh=fine,
        in_specs=(P(ROW, COL, None), out, P(), out, P(), P()),
        out_specs=(out,) * 5,
        check_vma=False,
    )
```

```python
import jax
import jax.numpy as jnp
from jax import lax
from jax.experimental import pallas as pl
from jax.experimental.pallas import tpu as pltpu
from jax.sharding import Mesh, PartitionSpec as P

ROW = ("x", "zh", "core")
COL = ("y", "zl")
ALL = ROW + COL
BF = jnp.bfloat16
F32 = jnp.float32
RING = (0, 1, 3, 2)


def dot(a, b, ca=1, cb=0):
    return lax.dot_general(a, b, (((ca,), (cb,)), ((), ())), preferred_element_type=F32)


def hold(a):
    return lax.optimization_barrier(a)


def exchange(a, axes):
    return lax.all_to_all(a, axes, 0, 0, tiled=True)


def shift(a, axis, by):
    n = lax.axis_size(axis)
    return lax.ppermute(a, axis, [(i, (i + by) % n) for i in range(n)])


def swap(a):
    return shift(a, "core", 1)


def ring(a, axis):
    return [a, shift(a, axis, -1), shift(a, axis, 1), shift(a, axis, 2)]


def lay_out(where, mine, others, panel, sems, blocks=range(4)):
    for n in blocks:
        for pieces, core in ((mine, where[2]), (others, 1 - where[2])):
            rows = pieces[0].shape[0] // 4
            for m, dz in enumerate(RING):
                piece, start = (pieces[n], m) if n < 3 else (pieces[3 + m // 2], m % 2)
                at = lax.rem(where[0] + RING[n], 4) * 4 + lax.rem(where[1] + dz, 4)
                at = pl.multiple_of((at * 2 + core) * rows, 32)
                pltpu.make_async_copy(
                    piece.at[pl.ds(start * rows, rows)], panel.at[pl.ds(at, rows)], sems.at[n]
                ).start()


def ring_block(n, where):
    return lax.rem(where[0] + RING[n], 4)


def near_kernel(where, *refs):
    z, out, panel, zcols, acc, sems, zsems, out_sem = refs[6:]
    depth = panel.shape[0] // 4

    def block(n):
        return pl.ds(pl.multiple_of(ring_block(n, where) * depth, 256), depth)

    zcopies = [pltpu.make_async_copy(z.at[:, block(n)], zcols.at[n], zsems.at[n]) for n in range(3)]
    for copy in zcopies:
        copy.start()
    lay_out(where, refs[:3], refs[3:6], panel, sems, range(3))
    for n in range(3):
        part = panel.at[block(n)]
        zcopies[n].wait()
        pltpu.make_async_copy(part, part, sems.at[n]).wait()
        got = jnp.dot(zcols[n], part[...], preferred_element_type=F32)
        if n == 0:
            acc[...] = got
        else:
            acc[...] += got
    copy = pltpu.make_async_copy(acc, out, out_sem)
    copy.start()
    copy.wait()


def far_kernel(where, *refs):
    near, z, out, own, panel, zcols, acc, result, sem, zsem, near_sem, out_sem, own_sem = refs[4:]
    depth, rows = panel.shape[0], refs[0].shape[0] // 2
    at = ring_block(3, where)
    zcopy = pltpu.make_async_copy(
        z.at[:, pl.ds(pl.multiple_of(at * depth, 256), depth)], zcols, zsem
    )
    zcopy.start()
    for pieces, core in ((refs[:2], where[2]), (refs[2:4], 1 - where[2])):
        for m, dz in enumerate(RING):
            to = pl.multiple_of((lax.rem(where[1] + dz, 4) * 2 + core) * rows, 32)
            pltpu.make_async_copy(
                pieces[m // 2].at[pl.ds(m % 2 * rows, rows)], panel.at[pl.ds(to, rows)], sem
            ).start()
    ncopy = pltpu.make_async_copy(near, acc, near_sem)
    ncopy.start()
    zcopy.wait()
    pltpu.make_async_copy(panel, panel, sem).wait()
    got = jnp.dot(zcols[...], panel[...], preferred_element_type=F32)
    ncopy.wait()
    got += acc[...]
    acc[...] = got
    result[...] = got.astype(BF).reshape(result.shape)
    copy = pltpu.make_async_copy(result, out, out_sem)
    copy.start()
    at = pl.multiple_of(where[3] * rows, 32)
    keep = pltpu.make_async_copy(acc.at[pl.ds(at, rows)], own, own_sem)
    keep.start()
    copy.wait()
    keep.wait()


def near_product(where, mine, others, z):
    depth, width = z.shape[1], mine[0].shape[1]
    hbm = pl.BlockSpec(memory_space=pltpu.HBM)
    return pl.pallas_call(
        near_kernel,
        grid_spec=pltpu.PrefetchScalarGridSpec(
            num_scalar_prefetch=1,
            grid=(),
            in_specs=[hbm] * 7,
            out_specs=hbm,
            scratch_shapes=[
                pltpu.VMEM((depth, width), BF),
                pltpu.VMEM((3, z.shape[0], depth // 4), BF),
                pltpu.VMEM((z.shape[0], width), F32),
                pltpu.SemaphoreType.DMA((3,)),
                pltpu.SemaphoreType.DMA((3,)),
                pltpu.SemaphoreType.DMA(()),
            ],
        ),
        out_shape=jax.ShapeDtypeStruct((z.shape[0], width), F32),
        compiler_params=pltpu.CompilerParams(vmem_limit_bytes=24 << 20),
        cost_estimate=pl.CostEstimate(
            flops=3 * z.size * width // 2,
            transcendentals=0,
            bytes_accessed=3 * z.size // 2 + 3 * depth * width // 2 + 4 * z.shape[0] * width,
        ),
    )(where, *mine, *others, z)


def far_product(where, mine, others, near, z, rows):
    depth, width = z.shape[1] // 4, near.shape[1]
    hbm = pl.BlockSpec(memory_space=pltpu.HBM)
    blocks = (z.shape[0] // rows, rows, width)
    return pl.pallas_call(
        far_kernel,
        grid_spec=pltpu.PrefetchScalarGridSpec(
            num_scalar_prefetch=1,
            grid=(),
            in_specs=[hbm] * 6,
            out_specs=[hbm] * 2,
            scratch_shapes=[
                pltpu.VMEM((depth, width), BF),
                pltpu.VMEM((z.shape[0], depth), BF),
                pltpu.VMEM((z.shape[0], width), F32),
                pltpu.VMEM(blocks, BF),
                pltpu.SemaphoreType.DMA(()),
                pltpu.SemaphoreType.DMA(()),
                pltpu.SemaphoreType.DMA(()),
                pltpu.SemaphoreType.DMA(()),
                pltpu.SemaphoreType.DMA(()),
            ],
        ),
        out_shape=[jax.ShapeDtypeStruct(blocks, BF), jax.ShapeDtypeStruct((rows, width), F32)],
        compiler_params=pltpu.CompilerParams(vmem_limit_bytes=24 << 20),
        cost_estimate=pl.CostEstimate(
            flops=z.size * width // 2,
            transcendentals=0,
            bytes_accessed=z.size // 2 + 2 * depth * width + 6 * z.shape[0] * width,
        ),
    )(where, *mine, *others, near, z)


def panel_kernel(where, *refs):
    out, panel, sems, out_sem = refs[10:]
    depth = panel.shape[0] // 4
    lay_out(where, refs[:5], refs[5:10], panel, sems)
    copies = []
    for step in range(4):
        at = pl.ds(pl.multiple_of(ring_block(step, where) * depth, 256), depth)
        pltpu.make_async_copy(panel.at[at], panel.at[at], sems.at[step]).wait()
        copies.append(pltpu.make_async_copy(panel.at[at], out.at[at], out_sem.at[step]))
        copies[-1].start()
    for copy in copies:
        copy.wait()


def whole_panel(where, mine, others, depth):
    width = mine[0].shape[1]
    hbm = pl.BlockSpec(memory_space=pltpu.HBM)
    return pl.pallas_call(
        panel_kernel,
        grid_spec=pltpu.PrefetchScalarGridSpec(
            num_scalar_prefetch=1,
            grid=(),
            in_specs=[hbm] * 10,
            out_specs=hbm,
            scratch_shapes=[
                pltpu.VMEM((depth, width), BF),
                pltpu.SemaphoreType.DMA((4,)),
                pltpu.SemaphoreType.DMA((4,)),
            ],
        ),
        out_shape=jax.ShapeDtypeStruct((depth, width), BF),
        compiler_params=pltpu.CompilerParams(vmem_limit_bytes=60 << 20),
        cost_estimate=pl.CostEstimate(flops=0, transcendentals=0, bytes_accessed=4 * depth * width),
    )(where, *mine, *others)


def slices_kernel(x, parent, child, cp, t, r, xt, pbuf, cbuf, cpbuf, big, psem, csem, cpsem):
    nr, kinds, sl, rows = x.shape
    depth, w = parent.shape
    parts = psem.shape[0]
    chunk = depth // parts
    copies = []
    for n in range(parts):
        at = pl.ds(n * chunk, chunk)
        copies.append((pltpu.make_async_copy(parent.at[at], pbuf.at[at], psem.at[n]), pltpu.make_async_copy(child.at[at], cbuf.at[at], csem.at[n])))
        for c in copies[-1]:
            c.start()
    ccopy = pltpu.make_async_copy(cp, cpbuf, cpsem)
    ccopy.start()
    for s in range(nr):
        xt[:, s * rows : (s + 1) * rows] = x[s].reshape(kinds * sl, rows)
    for n in range(parts):
        at = pl.ds(n * chunk, chunk)
        for c in copies[n]:
            c.wait()
        lhs = xt[:, n * chunk : (n + 1) * chunk]
        gp = jnp.dot(lhs[: 2 * sl], pbuf[at, :], preferred_element_type=F32)
        gc = jnp.dot(lhs, cbuf[at, :], preferred_element_type=F32)
        if n == 0:
            big[: 2 * sl] = gp
            big[2 * sl :] = gc
        else:
            big[: 2 * sl] += gp
            big[2 * sl :] += gc
    ccopy.wait()
    r[0] = big[2 * sl : 3 * sl]
    r[1] = big[3 * sl : 4 * sl]
    t2 = jnp.dot(big[sl : 2 * sl].astype(BF), cpbuf[...], preferred_element_type=F32) + big[4 * sl :]
    big[sl : 2 * sl] = t2
    lane = lax.broadcasted_iota(jnp.int32, (16, 128), 1) // sl
    for q in range(w // 128):
        for d in range(4):
            out = None
            for g in range(4):
                v = big[g * 16 : (g + 1) * 16, q * 128 : (q + 1) * 128]
                v = pltpu.roll(v, ((g - d) * sl) % 128, 1) if g != d else v
                out = v if out is None else jnp.where(lane == g, v, out)
            t[q * 4 + d] = out.astype(BF)

def slices(x, parent, child, cp):
    nr, kinds, sl, rows = x.shape
    depth, w = parent.shape
    parts = 4
    any_ = pl.BlockSpec(memory_space=pl.ANY)
    vm = pl.BlockSpec(memory_space=pltpu.VMEM)
    return pl.pallas_call(
        slices_kernel,
        in_specs=[vm, any_, any_, any_],
        out_specs=[vm, vm],
        out_shape=[jax.ShapeDtypeStruct((nr, 16, 128), BF), jax.ShapeDtypeStruct((2, sl, w), F32)],
        scratch_shapes=[pltpu.VMEM((kinds * sl, depth), BF), pltpu.VMEM((depth, w), BF), pltpu.VMEM((depth, w), BF), pltpu.VMEM(cp.shape, BF), pltpu.VMEM((5 * sl, w), F32),
            pltpu.SemaphoreType.DMA((parts,)), pltpu.SemaphoreType.DMA((parts,)), pltpu.SemaphoreType.DMA(())],
        compiler_params=pltpu.CompilerParams(vmem_limit_bytes=52 << 20),
        cost_estimate=pl.CostEstimate(flops=10 * sl * depth * w, transcendentals=0, bytes_accessed=4 * depth * w),
    )(x, parent, child, cp)

def rows_kernel(t, r, f, both):
    nr = t.shape[0]
    sl = r.shape[1]
    w = r.shape[2]
    for q in range(nr // 4):
        for kind in range(2):
            tall = []
            for d in range(4):
                for h in range(2):
                    v = t[q * 4 + d].astype(F32)
                    g = kind * 2 + h
                    tall.append(pltpu.roll(v, (128 - g * sl) % 128, 1) if g else v)
            tall = jnp.concatenate(tall, axis=0)
            both[kind, :, q * 128 : (q + 1) * 128] = tall.T[:sl]
    nc = f.shape[0]
    own = sl // nc
    half = w // 2
    for c in range(nc):
        at = slice(c * own, (c + 1) * own)
        low = both[1, at, :] - r[1, at, :]
        f[c, :own, :w] = both[0, at, :]
        f[c, own:, :w] = r[0, at, :]
        f[c, :own, w:] = low[:, :half]
        f[c, own:, w:] = low[:, half:]

def rows_of(t, r, nc):
    sl, w = r.shape[1:]
    vm = pl.BlockSpec(memory_space=pltpu.VMEM)
    return pl.pallas_call(
        rows_kernel, in_specs=[vm, vm], out_specs=vm,
        out_shape=jax.ShapeDtypeStruct((nc, 2 * sl // nc, 3 * w // 2), F32),
        scratch_shapes=[pltpu.VMEM((2, sl, w), F32)],
        compiler_params=pltpu.CompilerParams(vmem_limit_bytes=16 << 20),
        cost_estimate=pl.CostEstimate(flops=0, transcendentals=0, bytes_accessed=20 * sl * w),
    )(t, r)


def ancestors_kernel(where, got, own, shifted, ut, st, anc, x):
    nr, _, sl, rows = x.shape
    low = own[...] - shifted[...]
    for n in range(got.shape[0]):
        low += jnp.where(where[3] == n, 0.0, got[n].astype(F32))
    anc[...] = -low
    x[:, 0] = ut[...].reshape(nr, sl, rows)
    x[:, 1] = st[...].reshape(nr, sl, rows)
    x[:, 2] = low.T.astype(BF).reshape(nr, sl, rows)


def ancestors(where, got, own, shifted, ut, st, nr):
    rows, w = shifted.shape
    vmem = pl.BlockSpec(memory_space=pltpu.VMEM)
    return pl.pallas_call(
        ancestors_kernel,
        in_specs=[pl.BlockSpec(memory_space=pltpu.SMEM)] + [vmem] * 5,
        out_specs=[vmem] * 2,
        out_shape=[
            jax.ShapeDtypeStruct((rows, w), F32),
            jax.ShapeDtypeStruct((nr, 3, w // nr, rows), BF),
        ],
        compiler_params=pltpu.CompilerParams(vmem_limit_bytes=16 << 20),
        cost_estimate=pl.CostEstimate(flops=9 * rows * w, transcendentals=0, bytes_accessed=40 * rows * w),
    )(where, got, own, shifted, ut, st)


def shards(z, pp, pdi, ca, cp, cdi):
    rows, w = pp.shape
    nr, nc = lax.axis_size(ROW), lax.axis_size(COL)
    sl = w // nr
    own = sl // nc
    where = jnp.stack([lax.axis_index(a) for a in ROW + (COL,)]).astype(jnp.int32)
    block = z.reshape(z.shape[0], -1)

    child = lax.all_gather(ca, ROW, axis=0, tiled=True)
    diag_prod = dot(pdi, cp).astype(BF)
    first = (lax.axis_index(ROW) * nc + lax.axis_index(COL)) * own
    cols = lambda m: lax.dynamic_slice_in_dim(m, first, own, 1)
    diag_upper = dot(cols(pdi), pdi, 0, 0)
    diag_lower = dot(cols(cdi), cdi, 0, 0) + dot(cols(diag_prod), diag_prod, 0, 0)

    here = jnp.concatenate(ring(pp, "zh"))
    here, diag_upper, diag_lower = hold((here, diag_upper, diag_lower))
    after, before, here_other = hold((shift(here, "x", -1), shift(here, "x", 1), swap(here)))
    half = here.shape[0] // 2
    pieces = [here, after, before, shift(after[:half], "x", -1), shift(before[half:], "x", 1)]
    others = [here_other, swap(after), swap(before)]
    near = near_product(where, pieces[:3], others, block)
    pieces[3], pieces[4], near = hold((pieces[3], pieces[4], near))
    others += [swap(pieces[3]), swap(pieces[4])]
    up, own_up = far_product(where, pieces[3:], others[3:], near, block, rows)
    foreign = (jnp.arange(nc) != where[3])[:, None, None]
    upper = own_up + jnp.sum(jnp.where(foreign, exchange(up, COL).astype(F32), 0.0), axis=0)
    u = upper.astype(BF)
    shifted = dot(u, cp)
    s = shifted.astype(BF)

    lp = dot(block, child).astype(BF).reshape(nc, rows, w)
    got = exchange(lp, COL)
    own_lp = dot(lax.dynamic_slice_in_dim(block, where[3] * rows, rows, 0), child)
    anc, x = ancestors(where, got, own_lp, shifted, u.T, s.T, nr)
    others[0], x = hold((others[0], x))
    x = exchange(x, ROW)
    parent = whole_panel(where, pieces, others, block.shape[1])
    t, r = slices(x, parent, child, cp)
    t = exchange(t, ROW)
    f = jnp.sum(exchange(rows_of(t, r, nc), COL), axis=0)

    pp_out = diag_upper + f[:own, :w]
    pc = f[own:, :w] - dot(pp_out.astype(BF), cp)
    cc = diag_lower + jnp.concatenate([f[:own, w:], f[own:, w:]], axis=1)
    return -upper, pp_out, anc, pc, cc


def solution(mesh):
    fine = Mesh(mesh.devices.reshape(4, 4, 2, 4, 2), ALL)
    out = P(ALL, None)
    return jax.shard_map(
        shards,
        mesh=fine,
        in_specs=(P(ROW, COL, None), out, P(), out, P(), P()),
        out_specs=(out,) * 5,
        check_vma=False,
    )
```

```python
import jax
import jax.numpy as jnp
from jax import lax
from jax.experimental import pallas as pl
from jax.experimental.pallas import tpu as pltpu
from jax.sharding import Mesh, PartitionSpec as P

ROW = ("x", "zh", "core")
COL = ("y", "zl")
ALL = ROW + COL
BF = jnp.bfloat16
F32 = jnp.float32
RING = (0, 1, 3, 2)


def dot(a, b, ca=1, cb=0):
    return lax.dot_general(a, b, (((ca,), (cb,)), ((), ())), preferred_element_type=F32)


def hold(a):
    return lax.optimization_barrier(a)


def exchange(a, axes):
    return lax.all_to_all(a, axes, 0, 0, tiled=True)


def shift(a, axis, by):
    n = lax.axis_size(axis)
    return lax.ppermute(a, axis, [(i, (i + by) % n) for i in range(n)])


def swap(a):
    return shift(a, "core", 1)


def ring(a, axis):
    return [a, shift(a, axis, -1), shift(a, axis, 1), shift(a, axis, 2)]


def lay_out(where, mine, others, panel, sems, blocks=range(4)):
    for n in blocks:
        for pieces, core in ((mine, where[2]), (others, 1 - where[2])):
            rows = pieces[0].shape[0] // 4
            for m, dz in enumerate(RING):
                piece, start = (pieces[n], m) if n < 3 else (pieces[3 + m // 2], m % 2)
                at = lax.rem(where[0] + RING[n], 4) * 4 + lax.rem(where[1] + dz, 4)
                at = pl.multiple_of((at * 2 + core) * rows, 32)
                pltpu.make_async_copy(
                    piece.at[pl.ds(start * rows, rows)], panel.at[pl.ds(at, rows)], sems.at[n]
                ).start()


def ring_block(n, where):
    return lax.rem(where[0] + RING[n], 4)


def near_kernel(where, *refs):
    z, out, panel, zcols, acc, sems, zsems, out_sem = refs[6:]
    depth = panel.shape[0] // 4

    def block(n):
        return pl.ds(pl.multiple_of(ring_block(n, where) * depth, 256), depth)

    zcopies = [pltpu.make_async_copy(z.at[:, block(n)], zcols.at[n], zsems.at[n]) for n in range(3)]
    for copy in zcopies:
        copy.start()
    lay_out(where, refs[:3], refs[3:6], panel, sems, range(3))
    for n in range(3):
        part = panel.at[block(n)]
        zcopies[n].wait()
        pltpu.make_async_copy(part, part, sems.at[n]).wait()
        got = jnp.dot(zcols[n], part[...], preferred_element_type=F32)
        if n == 0:
            acc[...] = got
        else:
            acc[...] += got
    copy = pltpu.make_async_copy(acc, out, out_sem)
    copy.start()
    copy.wait()


def far_kernel(where, *refs):
    near, z, out, own, panel, zcols, acc, result, sem, zsem, near_sem, out_sem, own_sem = refs[4:]
    depth, rows = panel.shape[0], refs[0].shape[0] // 2
    at = ring_block(3, where)
    zcopy = pltpu.make_async_copy(
        z.at[:, pl.ds(pl.multiple_of(at * depth, 256), depth)], zcols, zsem
    )
    zcopy.start()
    for pieces, core in ((refs[:2], where[2]), (refs[2:4], 1 - where[2])):
        for m, dz in enumerate(RING):
            to = pl.multiple_of((lax.rem(where[1] + dz, 4) * 2 + core) * rows, 32)
            pltpu.make_async_copy(
                pieces[m // 2].at[pl.ds(m % 2 * rows, rows)], panel.at[pl.ds(to, rows)], sem
            ).start()
    ncopy = pltpu.make_async_copy(near, acc, near_sem)
    ncopy.start()
    zcopy.wait()
    pltpu.make_async_copy(panel, panel, sem).wait()
    got = jnp.dot(zcols[...], panel[...], preferred_element_type=F32)
    ncopy.wait()
    got += acc[...]
    acc[...] = got
    result[...] = got.astype(BF).reshape(result.shape)
    copy = pltpu.make_async_copy(result, out, out_sem)
    copy.start()
    at = pl.multiple_of(where[3] * rows, 32)
    keep = pltpu.make_async_copy(acc.at[pl.ds(at, rows)], own, own_sem)
    keep.start()
    copy.wait()
    keep.wait()


def near_product(where, mine, others, z):
    depth, width = z.shape[1], mine[0].shape[1]
    hbm = pl.BlockSpec(memory_space=pltpu.HBM)
    return pl.pallas_call(
        near_kernel,
        grid_spec=pltpu.PrefetchScalarGridSpec(
            num_scalar_prefetch=1,
            grid=(),
            in_specs=[hbm] * 7,
            out_specs=hbm,
            scratch_shapes=[
                pltpu.VMEM((depth, width), BF),
                pltpu.VMEM((3, z.shape[0], depth // 4), BF),
                pltpu.VMEM((z.shape[0], width), F32),
                pltpu.SemaphoreType.DMA((3,)),
                pltpu.SemaphoreType.DMA((3,)),
                pltpu.SemaphoreType.DMA(()),
            ],
        ),
        out_shape=jax.ShapeDtypeStruct((z.shape[0], width), F32),
        compiler_params=pltpu.CompilerParams(vmem_limit_bytes=24 << 20),
        cost_estimate=pl.CostEstimate(
            flops=3 * z.size * width // 2,
            transcendentals=0,
            bytes_accessed=3 * z.size // 2 + 3 * depth * width // 2 + 4 * z.shape[0] * width,
        ),
    )(where, *mine, *others, z)


def far_product(where, mine, others, near, z, rows):
    depth, width = z.shape[1] // 4, near.shape[1]
    hbm = pl.BlockSpec(memory_space=pltpu.HBM)
    blocks = (z.shape[0] // rows, rows, width)
    return pl.pallas_call(
        far_kernel,
        grid_spec=pltpu.PrefetchScalarGridSpec(
            num_scalar_prefetch=1,
            grid=(),
            in_specs=[hbm] * 6,
            out_specs=[hbm] * 2,
            scratch_shapes=[
                pltpu.VMEM((depth, width), BF),
                pltpu.VMEM((z.shape[0], depth), BF),
                pltpu.VMEM((z.shape[0], width), F32),
                pltpu.VMEM(blocks, BF),
                pltpu.SemaphoreType.DMA(()),
                pltpu.SemaphoreType.DMA(()),
                pltpu.SemaphoreType.DMA(()),
                pltpu.SemaphoreType.DMA(()),
                pltpu.SemaphoreType.DMA(()),
            ],
        ),
        out_shape=[jax.ShapeDtypeStruct(blocks, BF), jax.ShapeDtypeStruct((rows, width), F32)],
        compiler_params=pltpu.CompilerParams(vmem_limit_bytes=24 << 20),
        cost_estimate=pl.CostEstimate(
            flops=z.size * width // 2,
            transcendentals=0,
            bytes_accessed=z.size // 2 + 2 * depth * width + 6 * z.shape[0] * width,
        ),
    )(where, *mine, *others, near, z)


def panel_kernel(where, *refs):
    out, panel, sems, out_sem = refs[10:]
    depth = panel.shape[0] // 4
    lay_out(where, refs[:5], refs[5:10], panel, sems)
    copies = []
    for step in range(4):
        at = pl.ds(pl.multiple_of(ring_block(step, where) * depth, 256), depth)
        pltpu.make_async_copy(panel.at[at], panel.at[at], sems.at[step]).wait()
        copies.append(pltpu.make_async_copy(panel.at[at], out.at[at], out_sem.at[step]))
        copies[-1].start()
    for copy in copies:
        copy.wait()


def whole_panel(where, mine, others, depth):
    width = mine[0].shape[1]
    hbm = pl.BlockSpec(memory_space=pltpu.HBM)
    return pl.pallas_call(
        panel_kernel,
        grid_spec=pltpu.PrefetchScalarGridSpec(
            num_scalar_prefetch=1,
            grid=(),
            in_specs=[hbm] * 10,
            out_specs=hbm,
            scratch_shapes=[
                pltpu.VMEM((depth, width), BF),
                pltpu.SemaphoreType.DMA((4,)),
                pltpu.SemaphoreType.DMA((4,)),
            ],
        ),
        out_shape=jax.ShapeDtypeStruct((depth, width), BF),
        compiler_params=pltpu.CompilerParams(vmem_limit_bytes=60 << 20),
        cost_estimate=pl.CostEstimate(flops=0, transcendentals=0, bytes_accessed=4 * depth * width),
    )(where, *mine, *others)


def slices_kernel(x, parent, child, cp, t, r, xt, pbuf, cbuf, cpbuf, big, psem, csem, cpsem):
    nr, kinds, sl, rows = x.shape
    depth, w = parent.shape
    parts = psem.shape[0]
    chunk = depth // parts
    copies = []
    for n in range(parts):
        at = pl.ds(n * chunk, chunk)
        copies.append((pltpu.make_async_copy(parent.at[at], pbuf.at[at], psem.at[n]), pltpu.make_async_copy(child.at[at], cbuf.at[at], csem.at[n])))
        for c in copies[-1]:
            c.start()
    ccopy = pltpu.make_async_copy(cp, cpbuf, cpsem)
    ccopy.start()
    for s in range(nr):
        xt[:, s * rows : (s + 1) * rows] = x[s].reshape(kinds * sl, rows)
    for n in range(parts):
        at = pl.ds(n * chunk, chunk)
        for c in copies[n]:
            c.wait()
        lhs = xt[:, n * chunk : (n + 1) * chunk]
        gp = jnp.dot(lhs[: 2 * sl], pbuf[at, :], preferred_element_type=F32)
        gc = jnp.dot(lhs, cbuf[at, :], preferred_element_type=F32)
        if n == 0:
            big[: 2 * sl] = gp
            big[2 * sl :] = gc
        else:
            big[: 2 * sl] += gp
            big[2 * sl :] += gc
    ccopy.wait()
    r[0] = big[2 * sl : 3 * sl]
    r[1] = big[3 * sl : 4 * sl]
    t2 = jnp.dot(big[sl : 2 * sl].astype(BF), cpbuf[...], preferred_element_type=F32) + big[4 * sl :]
    big[sl : 2 * sl] = t2
    lane = lax.broadcasted_iota(jnp.int32, (16, 128), 1) // sl
    for q in range(w // 128):
        for d in range(4):
            out = None
            for g in range(4):
                v = big[g * 16 : (g + 1) * 16, q * 128 : (q + 1) * 128]
                v = pltpu.roll(v, ((g - d) * sl) % 128, 1) if g != d else v
                out = v if out is None else jnp.where(lane == g, v, out)
            t[q * 4 + d] = out.astype(BF)

def slices(x, parent, child, cp):
    nr, kinds, sl, rows = x.shape
    depth, w = parent.shape
    parts = 4
    any_ = pl.BlockSpec(memory_space=pl.ANY)
    vm = pl.BlockSpec(memory_space=pltpu.VMEM)
    return pl.pallas_call(
        slices_kernel,
        in_specs=[vm, any_, any_, any_],
        out_specs=[vm, vm],
        out_shape=[jax.ShapeDtypeStruct((nr, 16, 128), BF), jax.ShapeDtypeStruct((2, sl, w), F32)],
        scratch_shapes=[pltpu.VMEM((kinds * sl, depth), BF), pltpu.VMEM((depth, w), BF), pltpu.VMEM((depth, w), BF), pltpu.VMEM(cp.shape, BF), pltpu.VMEM((5 * sl, w), F32),
            pltpu.SemaphoreType.DMA((parts,)), pltpu.SemaphoreType.DMA((parts,)), pltpu.SemaphoreType.DMA(())],
        compiler_params=pltpu.CompilerParams(vmem_limit_bytes=52 << 20),
        cost_estimate=pl.CostEstimate(flops=10 * sl * depth * w, transcendentals=0, bytes_accessed=4 * depth * w),
    )(x, parent, child, cp)

def rows_kernel(t, r, f, both):
    nr = t.shape[0]
    sl = r.shape[1]
    w = r.shape[2]
    for q in range(nr // 4):
        for kind in range(2):
            tall = []
            for d in range(4):
                for h in range(2):
                    v = t[q * 4 + d].astype(F32)
                    g = kind * 2 + h
                    tall.append(pltpu.roll(v, (128 - g * sl) % 128, 1) if g else v)
            tall = jnp.concatenate(tall, axis=0)
            both[kind, :, q * 128 : (q + 1) * 128] = tall.T[:sl]
    nc = f.shape[0]
    own = sl // nc
    half = w // 2
    for c in range(nc):
        at = slice(c * own, (c + 1) * own)
        low = both[1, at, :] - r[1, at, :]
        f[c, :own, :w] = both[0, at, :]
        f[c, own:, :w] = r[0, at, :]
        f[c, :own, w:] = low[:, :half]
        f[c, own:, w:] = low[:, half:]

def rows_of(t, r, nc):
    sl, w = r.shape[1:]
    vm = pl.BlockSpec(memory_space=pltpu.VMEM)
    return pl.pallas_call(
        rows_kernel, in_specs=[vm, vm], out_specs=vm,
        out_shape=jax.ShapeDtypeStruct((nc, 2 * sl // nc, 3 * w // 2), F32),
        scratch_shapes=[pltpu.VMEM((2, sl, w), F32)],
        compiler_params=pltpu.CompilerParams(vmem_limit_bytes=16 << 20),
        cost_estimate=pl.CostEstimate(flops=0, transcendentals=0, bytes_accessed=20 * sl * w),
    )(t, r)


def ancestors_kernel(where, got, own, shifted, ut, st, anc, x):
    nr, _, sl, rows = x.shape
    low = own[...] - shifted[...]
    for n in range(got.shape[0]):
        low += jnp.where(where[3] == n, 0.0, got[n].astype(F32))
    anc[...] = -low
    x[:, 0] = ut[...].reshape(nr, sl, rows)
    x[:, 1] = st[...].reshape(nr, sl, rows)
    x[:, 2] = low.T.astype(BF).reshape(nr, sl, rows)


def ancestors(where, got, own, shifted, ut, st, nr):
    rows, w = shifted.shape
    vmem = pl.BlockSpec(memory_space=pltpu.VMEM)
    return pl.pallas_call(
        ancestors_kernel,
        in_specs=[pl.BlockSpec(memory_space=pltpu.SMEM)] + [vmem] * 5,
        out_specs=[vmem] * 2,
        out_shape=[
            jax.ShapeDtypeStruct((rows, w), F32),
            jax.ShapeDtypeStruct((nr, 3, w // nr, rows), BF),
        ],
        compiler_params=pltpu.CompilerParams(vmem_limit_bytes=54 << 20),
        cost_estimate=pl.CostEstimate(flops=9 * rows * w, transcendentals=0, bytes_accessed=40 * rows * w),
    )(where, got, own, shifted, ut, st)


def shards(z, pp, pdi, ca, cp, cdi):
    rows, w = pp.shape
    nr, nc = lax.axis_size(ROW), lax.axis_size(COL)
    sl = w // nr
    own = sl // nc
    where = jnp.stack([lax.axis_index(a) for a in ROW + (COL,)]).astype(jnp.int32)
    block = z.reshape(z.shape[0], -1)

    child = lax.all_gather(ca, ROW, axis=0, tiled=True)
    diag_prod = dot(pdi, cp).astype(BF)
    first = (lax.axis_index(ROW) * nc + lax.axis_index(COL)) * own
    cols = lambda m: lax.dynamic_slice_in_dim(m, first, own, 1)
    diag_upper = dot(cols(pdi), pdi, 0, 0)
    diag_lower = dot(cols(cdi), cdi, 0, 0) + dot(cols(diag_prod), diag_prod, 0, 0)

    here = jnp.concatenate(ring(pp, "zh"))
    here, diag_upper, diag_lower = hold((here, diag_upper, diag_lower))
    after, before, here_other = hold((shift(here, "x", -1), shift(here, "x", 1), swap(here)))
    half = here.shape[0] // 2
    pieces = [here, after, before, shift(after[:half], "x", -1), shift(before[half:], "x", 1)]
    others = [here_other, swap(after), swap(before)]
    near = near_product(where, pieces[:3], others, block)
    pieces[3], pieces[4], near = hold((pieces[3], pieces[4], near))
    others += [swap(pieces[3]), swap(pieces[4])]
    up, own_up = far_product(where, pieces[3:], others[3:], near, block, rows)
    foreign = (jnp.arange(nc) != where[3])[:, None, None]
    upper = own_up + jnp.sum(jnp.where(foreign, exchange(up, COL).astype(F32), 0.0), axis=0)
    u = upper.astype(BF)
    shifted = dot(u, cp)
    s = shifted.astype(BF)

    lp = dot(block, child).astype(BF).reshape(nc, rows, w)
    got = exchange(lp, COL)
    own_lp = dot(lax.dynamic_slice_in_dim(block, where[3] * rows, rows, 0), child)
    anc, x = ancestors(where, got, own_lp, shifted, u.T, s.T, nr)
    others[0], x = hold((others[0], x))
    x = exchange(x, ROW)
    parent = whole_panel(where, pieces, others, block.shape[1])
    t, r = slices(x, parent, child, cp)
    t = exchange(t, ROW)
    f = jnp.sum(exchange(rows_of(t, r, nc), COL), axis=0)

    pp_out = diag_upper + f[:own, :w]
    pc = f[own:, :w] - dot(pp_out.astype(BF), cp)
    cc = diag_lower + jnp.concatenate([f[:own, w:], f[own:, w:]], axis=1)
    return -upper, pp_out, anc, pc, cc


def solution(mesh):
    fine = Mesh(mesh.devices.reshape(4, 4, 2, 4, 2), ALL)
    out = P(ALL, None)
    return jax.shard_map(
        shards,
        mesh=fine,
        in_specs=(P(ROW, COL, None), out, P(), out, P(), P()),
        out_specs=(out,) * 5,
        check_vma=False,
    )
```
